512 devices in a mesh: shots: 128 (over z, y, core), sub: 4 (over x).
Axes of the slice: x: 4, y: 4, z: 16, core: 2. Of those that a mesh axis runs over, the one named last changes fastest.
Arguments:
- model: float32 [128, 512, 256], P('shots'), may hold values from 0.08 to 0.19
- anchor_x: int32 [128], replicated, may hold values from 0 to 496
- anchor_y: int32 [128], replicated, may hold values from 0 to 128
- state_before: bfloat16 [128, 128, 16, 128], P('shots', None, 'sub'), may hold values from -1.5 to 1.5
- state_now: bfloat16 [128, 128, 16, 128], P('shots', None, 'sub'), may hold values from -1.5 to 1.5
- adjoint_later: bfloat16 [128, 128, 16, 128], P('shots', None, 'sub'), may hold values from -1.5 to 1.5
- adjoint_latest: bfloat16 [128, 128, 16, 128], P('shots', None, 'sub'), may hold values from -1.5 to 1.5
- wavelet: float32 [128, 3], P('shots'), may hold values from -8 to 8
- src_index: int32 [128], P('shots'), may hold values from 0 to 262143
- rec_index: int32 [128, 512], P('shots'), may hold values from 0 to 262143
- observed: float32 [128, 3, 512], P('shots'), may hold values from -3 to 3
Outputs:
- gradient: float32 [128, 512, 256], P('shots', 'sub')
- adjoint_first: bfloat16 [128, 128, 16, 128], P('shots', None, 'sub')
- adjoint_second: bfloat16 [128, 128, 16, 128], P('shots', None, 'sub')
The draws below stay inside these ranges and needn't reach their ends.
All inputs are finite; a program needn't handle non-finite values.
Results may differ from the reference program's by a relative error of at most 0.001.
Values sent between devices are 32-bit elements; how exact they have to be, the bound alone decides.
No kernel may reach another device: no remote copies, remote signals or barrier semaphores. Data moves between devices by JAX's collectives and lax.ppermute only.
A program may use at most 64 MiB of HBM per device.

```python
import jax
import jax.numpy as jnp
from jax import lax

SX = 4
AY = 128
MX = 512
MY = 256
STEPS = 3
NREC = 512
Z = 128
AX = 16
SHOTS = 128
N_SUB = 4


def with_ends(drawn, key, smallest, high):
    longest = drawn.shape.index(max(drawn.shape))
    spots = []
    for shift in (0, 1):
        where = [jax.random.randint(jax.random.fold_in(key, axis), (), 0, length) for axis, length in enumerate(drawn.shape)]
        where[longest] = (where[longest] + shift) % drawn.shape[longest]
        spots.append(tuple(where))
    return drawn.at[spots[0]].set(smallest).at[spots[1]].set(high)


def block_scale(key, dims, pieces, low, top_value):
    def one(dim, parts):
        heights = jax.random.uniform(jax.random.fold_in(jax.random.fold_in(key, 6), dim), (parts,), jnp.float32, low / len(pieces), top_value / len(pieces))
        return jnp.repeat(jnp.exp(heights), dims[dim] // parts).reshape((-1,) + (1,) * (len(dims) - dim - 1))

    level = one(*pieces[0])
    for cut in pieces[1:]:
        level = level * one(*cut)
    return level


def normal_values(stream_key, dims, width, most, split=(), held_as=jnp.bfloat16):
    loudness = block_scale(stream_key, dims, split, -0.22, 0.18) if split else 1.0
    entries = jax.random.normal(stream_key, dims, jnp.float32) * width * loudness
    return jnp.minimum(jnp.maximum(entries, -most), most).astype(held_as)


def setup_inputs(seed: int = 0) -> dict:
    key_list = jax.random.split(jax.random.key(seed), 12)
    model = jnp.clip(0.08 + 0.11 * jax.random.uniform(key_list[0], (Z, MX, MY), jnp.float32) ** block_scale(key_list[0], (Z, MX, MY), ((0, 128),), -0.2, 0.2), 0.08, 0.19)
    anchor_x = with_ends(jax.random.randint(key_list[1], (SHOTS,), 0, MX - SX * N_SUB + 1), jax.random.fold_in(key_list[1], 1), 0, MX - SX * N_SUB).astype(jnp.int32)
    anchor_y = with_ends(jax.random.randint(key_list[2], (SHOTS,), 0, MY - AY + 1), jax.random.fold_in(key_list[2], 1), 0, MY - AY).astype(jnp.int32)
    state_before = normal_values(key_list[3], (SHOTS, Z, AX, AY), 0.25, 1.5, ((0, 128), (2, 4)))
    state_now = normal_values(key_list[4], (SHOTS, Z, AX, AY), 0.25, 1.5, ((0, 128), (2, 4)))
    adjoint_later = normal_values(key_list[5], (SHOTS, Z, AX, AY), 0.25, 1.5, ((0, 128), (2, 4)))
    adjoint_latest = normal_values(key_list[6], (SHOTS, Z, AX, AY), 0.25, 1.5, ((0, 128), (2, 4)))
    wavelet = normal_values(key_list[7], (SHOTS, STEPS), 2.0, 8.0, ((0, 128),), jnp.float32)
    src_index = with_ends(jax.random.randint(key_list[8], (SHOTS,), 0, Z * SX * N_SUB * AY), jax.random.fold_in(key_list[8], 1), 0, (Z * SX * N_SUB * AY) - 1).astype(jnp.int32)
    rec_index = with_ends(jax.random.randint(key_list[9], (SHOTS, NREC), 0, Z * SX * N_SUB * AY), jax.random.fold_in(key_list[9], 1), 0, (Z * SX * N_SUB * AY) - 1).astype(jnp.int32)
    observed = normal_values(key_list[10], (SHOTS, STEPS, NREC), 0.5, 3.0, ((0, 128),), jnp.float32)
    return dict(model=model, anchor_x=anchor_x, anchor_y=anchor_y, state_before=state_before, state_now=state_now, adjoint_later=adjoint_later, adjoint_latest=adjoint_latest, wavelet=wavelet, src_index=src_index, rec_index=rec_index, observed=observed)


STENCIL = (-205.0 / 72.0, 8.0 / 5.0, -1.0 / 5.0, 8.0 / 315.0, -1.0 / 560.0)


def laplace(field):
    depth, inner_x, inner_y = field.shape
    padded = jnp.pad(field, 4)

    def window(shift_z, shift_x, shift_y):
        return padded[4 + shift_z:4 + shift_z + depth, 4 + shift_x:4 + shift_x + inner_x, 4 + shift_y:4 + shift_y + inner_y]

    total = 3.0 * STENCIL[0] * window(0, 0, 0)
    for reach in range(1, 5):
        near = window(reach, 0, 0) + window(-reach, 0, 0)
        near = near + window(0, reach, 0) + window(0, -reach, 0)
        near = near + window(0, 0, reach) + window(0, 0, -reach)
        total = total + STENCIL[reach] * near
    return total


def one_shot(model, start_x, start_y, before, now, later, latest, amplitude, source, receivers, recorded):
    speed = lax.dynamic_slice(model, (jnp.int32(0), start_x, start_y), (Z, SX * N_SUB, AY))
    previous = before.astype(jnp.float32)
    current = now.astype(jnp.float32)
    states = [current]
    for index in range(STEPS):
        following = 2.0 * current - previous + speed * laplace(current)
        following = following.reshape(-1).at[source].add(amplitude[index]).reshape(following.shape)
        previous, current = current, following
        states.append(following)
    adjoint_one = later.astype(jnp.float32)
    adjoint_two = latest.astype(jnp.float32)
    shot_grad = jnp.zeros(speed.shape, jnp.float32)
    for index in range(STEPS, 0, -1):
        adjoint = 2.0 * adjoint_one + laplace(speed * adjoint_one) - adjoint_two
        residual = states[index].reshape(-1)[receivers] - recorded[index - 1]
        adjoint = adjoint.reshape(-1).at[receivers].add(residual).reshape(adjoint.shape)
        shot_grad = shot_grad + adjoint * laplace(states[index - 1])
        adjoint_two, adjoint_one = adjoint_one, adjoint
    return shot_grad, adjoint_one, adjoint_two


def reference(model, anchor_x, anchor_y, state_before, state_now, adjoint_later, adjoint_latest, wavelet, src_index, rec_index, observed):
    def advance(total, inputs):
        start_x, start_y, before, now, later, latest, amplitude, source, receivers, recorded = inputs
        shot_grad, first, second = one_shot(model, start_x, start_y, before, now, later, latest, amplitude, source, receivers, recorded)
        corner = (jnp.int32(0), start_x, start_y)
        placed = lax.dynamic_slice(total, corner, shot_grad.shape) + shot_grad
        total = lax.dynamic_update_slice(total, placed, corner)
        return total, (first.astype(jnp.bfloat16), second.astype(jnp.bfloat16))

    inputs = (anchor_x, anchor_y, state_before, state_now, adjoint_later, adjoint_latest, wavelet, src_index, rec_index, observed)
    gradient, (adjoint_first, adjoint_second) = lax.scan(advance, jnp.zeros(model.shape, jnp.float32), inputs)
    return gradient, adjoint_first, adjoint_second
```

```python
import functools

import jax
import jax.numpy as jnp
import numpy as np
from jax import lax
from jax.experimental import pallas as pl
from jax.experimental.pallas import tpu as pltpu
from jax.sharding import PartitionSpec as P

STEPS = 3
REACH = 4
UNIT = 5040.0
WHOLE = (8064.0, -1008.0, 128.0, -9.0)
CENTRE = 3.0 * (-205.0 / 72.0)
WEIGHTS = (8.0 / 5.0, -1.0 / 5.0, 8.0 / 315.0, -1.0 / 560.0)

SMEM = pl.BlockSpec(memory_space=pltpu.SMEM)
VMEM = pl.BlockSpec(memory_space=pltpu.VMEM)
PARAMS = pltpu.CompilerParams(vmem_limit_bytes=44 << 20)


def band(size):
    offset = np.abs(np.arange(size)[:, None] - np.arange(size)[None, :])
    matrix = np.zeros((size, size), np.float32)
    for reach, weight in enumerate(WHOLE, start=1):
        matrix[offset == reach] = weight
    return jnp.asarray(matrix, jnp.bfloat16)


def laplace(ref, x, band_ref):
    centre = ref[x + REACH]
    high = centre.astype(jnp.bfloat16)
    low = (centre - high.astype(jnp.float32)).astype(jnp.bfloat16)
    weights = band_ref[...]
    along_y = jnp.dot(
        jnp.concatenate([high, low], axis=1),
        jnp.concatenate([weights, weights], axis=0),
        preferred_element_type=jnp.float32,
    )
    along_z = jnp.dot(
        jnp.concatenate([weights, weights], axis=1),
        jnp.concatenate([high, low], axis=0),
        preferred_element_type=jnp.float32,
    )
    total = CENTRE * centre + (along_y + along_z) * (1.0 / UNIT)
    for reach, weight in enumerate(WEIGHTS, start=1):
        total = total + weight * (ref[x + REACH - reach] + ref[x + REACH + reach])
    return total


def cut_kernel(shots, width_x, me_ref, ax_ref, ay_ref, model_ref, out_ref, near_ref, far_ref):
    width_y = out_ref.shape[1]
    first = me_ref[0] * width_x
    near_ref[...] = model_ref[:, :width_y]
    far_ref[...] = model_ref[:, width_y:]
    lane = lax.broadcasted_iota(jnp.int32, (width_x, width_y), 1)

    def body(shot, carry):
        rows = pl.ds(ax_ref[shot] + first, width_x)
        column = ay_ref[shot]
        turn = lax.rem(2 * width_y - column, width_y)
        near = pltpu.roll(near_ref[rows, :], turn, 1)
        far = pltpu.roll(far_ref[rows, :], turn, 1)
        start = pl.multiple_of(shot * width_x, width_x)
        out_ref[pl.ds(start, width_x), :] = jnp.where(lane < width_y - column, near, far)
        return carry

    lax.fori_loop(0, shots, body, 0, unroll=8)


def spread_kernel(shots, width_x, me_ref, ax_ref, ay_ref, in_ref, out_ref, near_ref, far_ref):
    width_y = in_ref.shape[1]
    first = me_ref[0] * width_x
    near_ref[...] = jnp.zeros_like(near_ref)
    far_ref[...] = jnp.zeros_like(far_ref)
    lane = lax.broadcasted_iota(jnp.int32, (width_x, width_y), 1)

    def body(shot, carry):
        start = pl.multiple_of(shot * width_x, width_x)
        column = ay_ref[shot]
        moved = pltpu.roll(in_ref[pl.ds(start, width_x), :], lax.rem(column, width_y), 1)
        rows = pl.ds(ax_ref[shot] + first, width_x)
        near_ref[rows, :] = near_ref[rows, :] + jnp.where(lane < column, 0.0, moved)
        far_ref[rows, :] = far_ref[rows, :] + jnp.where(lane < column, moved, 0.0)
        return carry

    lax.fori_loop(0, shots, body, 0, unroll=8)
    out_ref[:, :width_y] = near_ref[...]
    out_ref[:, width_y:] = far_ref[...]


def receiver_kernel(count, across, depth, index_ref, seen_ref, out_ref):
    width_y = out_ref.shape[2]
    out_ref[...] = jnp.zeros_like(out_ref)
    shape = out_ref.shape[1:]
    lane = lax.broadcasted_iota(jnp.int32, shape, 1)
    line = lax.broadcasted_iota(jnp.int32, shape, 0)

    def body(receiver, carry):
        flat = index_ref[receiver]
        cell_z = flat // (across * width_y)
        cell_x = flat // width_y % across
        cell_y = flat % width_y
        value = jnp.where(line == 1, seen_ref[0, receiver], 1.0)
        value = jnp.where(line == 2, seen_ref[1, receiver], value)
        value = jnp.where(line == 3, seen_ref[2, receiver], value)
        row = cell_x * depth + cell_z
        out_ref[row] = out_ref[row] + jnp.where(lane == cell_y, value, 0.0)
        return carry

    lax.fori_loop(0, count, body, 0, unroll=4)


def slab_slice(ref, first, depth, width_x, row):
    return ref[pl.ds(first + row, depth, stride=width_x), :]


def before_kernel(
    slabs, depth, width_x, me_ref, own_ref, left_ref, right_ref, far_a_ref, far_b_ref, band_ref,
    start_ref, push_ref, later_ref, back_ref, curve_ref, pad_ref,
):
    me = me_ref[0]
    block = depth * width_x
    outs = (start_ref, push_ref, later_ref, back_ref)
    for distance, pieces in (
        (0, [(own_ref, k) for k in range(4)]),
        (slabs - 1, [(left_ref, k) for k in range(4)]),
        (1, [(right_ref, k) for k in range(4)]),
        (2, [(far_a_ref, 0), (far_a_ref, 1), (far_b_ref, 0), (far_b_ref, 1)]),
    ):
        base = lax.rem(me + distance, slabs) * width_x
        for (ref, place), out in zip(pieces, outs):
            for row in range(width_x):
                out[base + row] = slab_slice(ref, place * block, depth, width_x, row)
    across = slabs * width_x
    zeros = jnp.zeros(pad_ref.shape[1:], jnp.float32)
    for row in range(REACH):
        pad_ref[row] = zeros
        pad_ref[REACH + across + row] = zeros

    def copy(x, carry):
        pad_ref[x + REACH] = start_ref[x]
        return carry

    lax.fori_loop(0, across, copy, 0)

    def curve(x, carry):
        curve_ref[x] = laplace(pad_ref, x, band_ref)
        return carry

    lax.fori_loop(0, across, curve, 0)


def main_kernel(
    slabs, depth, width_x, me_ref, source_ref, wave_ref, own_ref, left_ref, right_ref, far_ref,
    start_ref, push_ref, later_ref, back_ref, curve_ref, extra_ref, band_ref,
    grad_ref, first_ref, second_ref,
    speed_ref, one_ref, two_ref, scaled_ref, again_ref, curve_one_ref, lam_ref, lam_two_ref, sum_ref, mark_ref,
):
    me = me_ref[0]
    across = slabs * width_x
    width_y = mark_ref.shape[1]
    for distance, ref in ((0, own_ref), (slabs - 1, left_ref), (1, right_ref), (2, far_ref)):
        base = lax.rem(me + distance, slabs) * width_x
        for row in range(width_x):
            speed_ref[base + row] = slab_slice(ref, 0, depth, width_x, row)
    zeros = jnp.zeros((depth, width_y), jnp.float32)
    for ref in (one_ref, two_ref, scaled_ref, again_ref):
        for row in range(REACH):
            ref[row] = zeros
            ref[REACH + across + row] = zeros
    flat = source_ref[0]
    source_z = flat // (across * width_y)
    source_x = flat // width_y % across
    source_y = flat % width_y
    spot_z = lax.broadcasted_iota(jnp.int32, (depth, width_y), 0) == source_z
    spot_y = lax.broadcasted_iota(jnp.int32, (depth, width_y), 1) == source_y
    mark_ref[...] = jnp.where(spot_z & spot_y, 1.0, 0.0)

    def pulse(x, step):
        return mark_ref[...] * jnp.where(x == source_x, wave_ref[0, step], 0.0)

    def extra(x, line):
        return extra_ref[pl.ds(x * (depth * 4) + line, depth, stride=4), :]

    def step_one(x, carry):
        speed = speed_ref[x]
        one_ref[x + REACH] = push_ref[x] + speed * curve_ref[x] + pulse(x, 0)
        scaled_ref[x + REACH] = speed * later_ref[x]
        return carry

    lax.fori_loop(0, across, step_one, 0)

    def step_two(x, carry):
        bend = laplace(one_ref, x, band_ref)
        curve_one_ref[x] = bend
        two_ref[x + REACH] = 2.0 * one_ref[x + REACH] - start_ref[x] + speed_ref[x] * bend + pulse(x, 1)
        return carry

    lax.fori_loop(0, across, step_two, 0)

    def reach(slices):
        low = jnp.maximum(me * width_x - slices, 0)
        return low, jnp.minimum((me + 1) * width_x + slices, across)

    def back_three(x, carry):
        speed = speed_ref[x]
        bend = laplace(two_ref, x, band_ref)
        three = 2.0 * two_ref[x + REACH] - one_ref[x + REACH] + speed * bend + pulse(x, 2)
        lam = back_ref[x] + laplace(scaled_ref, x, band_ref)
        lam = lam + (extra(x, 0) * three - extra(x, 3))
        lam_ref[x] = lam
        sum_ref[x] = lam * bend
        again_ref[x + REACH] = speed * lam
        return carry

    low, high = reach(2 * REACH)
    lax.fori_loop(low, high, back_three, 0)

    def back_two(x, carry):
        lam = 2.0 * lam_ref[x] - later_ref[x] + laplace(again_ref, x, band_ref)
        lam = lam + (extra(x, 0) * two_ref[x + REACH] - extra(x, 2))
        lam_two_ref[x] = lam
        sum_ref[x] = sum_ref[x] + lam * curve_one_ref[x]
        scaled_ref[x + REACH] = speed_ref[x] * lam
        return carry

    low, high = reach(REACH)
    lax.fori_loop(low, high, back_two, 0)

    for row in range(width_x):
        x = me * width_x + row
        lam = 2.0 * lam_two_ref[x] - lam_ref[x] + laplace(scaled_ref, x, band_ref)
        lam = lam + (extra(x, 0) * one_ref[x + REACH] - extra(x, 1))
        first_ref[row] = lam.astype(first_ref.dtype)
        second_ref[row] = lam_two_ref[x].astype(second_ref.dtype)
        grad_ref[pl.ds(row, depth, stride=width_x), :] = sum_ref[x] + lam * curve_ref[x]


def shift(x, distance):
    count = lax.axis_size("sub")
    return lax.ppermute(x, "sub", [(i, (i + distance) % count) for i in range(count)])


def per_device(
    model,
    anchor_x,
    anchor_y,
    state_before,
    state_now,
    adjoint_later,
    adjoint_latest,
    wavelet,
    src_index,
    rec_index,
    observed,
):
    groups = lax.axis_size("shots")
    slabs = lax.axis_size("sub")
    _, model_x, model_y = model.shape
    depth, width_x, width_y = state_now.shape[1:]
    across = width_x * slabs
    block = depth * width_x
    me = lax.axis_index("sub").astype(jnp.int32)[None]
    weights = band(width_y)
    f32 = jnp.float32

    def shape(*dims):
        return jax.ShapeDtypeStruct(dims, f32)

    now = state_now[0].astype(f32)
    later = adjoint_later[0].astype(f32)
    fields = jnp.stack(
        [
            now,
            2.0 * now - state_before[0].astype(f32),
            later,
            2.0 * later - adjoint_latest[0].astype(f32),
        ]
    ).reshape(4 * block, width_y)
    left = shift(fields, 1)
    right = shift(fields, -1)
    far_a = shift(left[: 2 * block], 1)
    far_b = shift(right[2 * block :], -1)

    panels = pl.pallas_call(
        functools.partial(cut_kernel, groups, width_x),
        out_shape=shape(groups * width_x, width_y),
        in_specs=[SMEM, SMEM, SMEM, VMEM],
        out_specs=VMEM,
        scratch_shapes=[pltpu.VMEM((model_x, width_y), f32)] * 2,
        compiler_params=PARAMS,
        name="cut",
    )(me, anchor_x, anchor_y, model[0])
    speed = lax.all_to_all(
        panels.reshape(groups, width_x, width_y), "shots", split_axis=0, concat_axis=0, tiled=True
    ).reshape(block, width_y)

    extra = pl.pallas_call(
        functools.partial(receiver_kernel, rec_index.shape[1], across, depth),
        out_shape=shape(across * depth, 4, width_y),
        in_specs=[SMEM, SMEM],
        out_specs=VMEM,
        compiler_params=PARAMS,
        name="receivers",
    )(rec_index[0], observed[0]).reshape(across * depth * 4, width_y)

    whole = (across, depth, width_y)
    padded = (across + 2 * REACH, depth, width_y)
    start, push, late, back, curve = pl.pallas_call(
        functools.partial(before_kernel, slabs, depth, width_x),
        out_shape=[shape(*whole)] * 5,
        in_specs=[SMEM] + [VMEM] * 6,
        out_specs=[VMEM] * 5,
        scratch_shapes=[pltpu.VMEM(padded, f32)],
        compiler_params=PARAMS,
        name="before",
    )(me, fields, left, right, far_a, far_b, weights)

    speed_left = shift(speed, 1)
    speed_right = shift(speed, -1)
    speed_far = shift(speed, 2)

    slab = jax.ShapeDtypeStruct((width_x, depth, width_y), jnp.bfloat16)
    grad, first, second = pl.pallas_call(
        functools.partial(main_kernel, slabs, depth, width_x),
        out_shape=[shape(block, width_y), slab, slab],
        in_specs=[SMEM] * 3 + [VMEM] * 11,
        out_specs=[VMEM] * 3,
        scratch_shapes=[
            pltpu.VMEM(whole, f32),
            pltpu.VMEM(padded, f32),
            pltpu.VMEM(padded, f32),
            pltpu.VMEM(padded, f32),
            pltpu.VMEM(padded, f32),
            pltpu.VMEM(whole, f32),
            pltpu.VMEM(whole, f32),
            pltpu.VMEM(whole, f32),
            pltpu.VMEM(whole, f32),
            pltpu.VMEM((depth, width_y), f32),
        ],
        compiler_params=PARAMS,
        name="window",
    )(
        me, src_index, wavelet, speed, speed_left, speed_right, speed_far,
        start, push, late, back, curve, extra, weights,
    )

    returned = lax.all_to_all(
        grad.reshape(groups, width_x, width_y), "shots", split_axis=0, concat_axis=0, tiled=True
    ).reshape(groups * width_x, width_y)
    owned = pl.pallas_call(
        functools.partial(spread_kernel, groups, width_x),
        out_shape=shape(model_x, model_y),
        in_specs=[SMEM, SMEM, SMEM, VMEM],
        out_specs=VMEM,
        scratch_shapes=[pltpu.VMEM((model_x, width_y), f32)] * 2,
        compiler_params=PARAMS,
        name="spread",
    )(me, anchor_x, anchor_y, returned)
    parts = lax.all_to_all(
        owned.reshape(slabs, model_x // slabs, model_y), "sub", split_axis=0, concat_axis=0, tiled=True
    )
    gradient = parts[0]
    for index in range(1, slabs):
        gradient = gradient + parts[index]
    return (
        gradient[None],
        jnp.transpose(first, (1, 0, 2))[None],
        jnp.transpose(second, (1, 0, 2))[None],
    )


def solution(mesh):
    return jax.shard_map(
        per_device,
        mesh=mesh,
        in_specs=(
            P("shots", None, None),
            P(),
            P(),
            P("shots", None, "sub", None),
            P("shots", None, "sub", None),
            P("shots", None, "sub", None),
            P("shots", None, "sub", None),
            P("shots", None),
            P("shots"),
            P("shots", None),
            P("shots", None, None),
        ),
        out_specs=(
            P("shots", "sub", None),
            P("shots", None, "sub", None),
            P("shots", None, "sub", None),
        ),
        check_vma=False,
    )
```

```python
import functools

import jax
import jax.numpy as jnp
import numpy as np
from jax import lax
from jax.experimental import pallas as pl
from jax.experimental.pallas import tpu as pltpu
from jax.sharding import PartitionSpec as P

STEPS = 3
REACH = 4
UNIT = 5040.0
WHOLE = (8064.0, -1008.0, 128.0, -9.0)
CENTRE = 3.0 * (-205.0 / 72.0)
WEIGHTS = (8.0 / 5.0, -1.0 / 5.0, 8.0 / 315.0, -1.0 / 560.0)

SMEM = pl.BlockSpec(memory_space=pltpu.SMEM)
HBM = pl.BlockSpec(memory_space=pltpu.HBM)
VMEM = pl.BlockSpec(memory_space=pltpu.VMEM)
PARAMS = pltpu.CompilerParams(vmem_limit_bytes=24 << 20)


def band(size):
    offset = np.abs(np.arange(size)[:, None] - np.arange(size)[None, :])
    matrix = np.zeros((size, size), np.float32)
    for reach, weight in enumerate(WHOLE, start=1):
        matrix[offset == reach] = weight
    return jnp.asarray(matrix, jnp.bfloat16)


ROWS = 16


def along(ref, x, count, band_ref, part_ref):
    weights = band_ref[...]
    twice_down = jnp.concatenate([weights, weights], axis=0)
    twice_across = jnp.concatenate([weights, weights], axis=1)
    for index in range(count):
        centre = ref[x + REACH + index]
        high = centre.astype(jnp.bfloat16)
        low = (centre - high.astype(jnp.float32)).astype(jnp.bfloat16)
        along_y = jnp.dot(jnp.concatenate([high, low], axis=1), twice_down, preferred_element_type=jnp.float32)
        along_z = jnp.dot(twice_across, jnp.concatenate([high, low], axis=0), preferred_element_type=jnp.float32)
        part_ref[index] = along_y + along_z


def laplace(ref, x, count, rows, part_ref):
    near = [ref[x + index, rows, :] for index in range(count + 2 * REACH)]
    totals = []
    for index in range(count):
        centre = index + REACH
        total = CENTRE * near[centre] + part_ref[index, rows, :] * (1.0 / UNIT)
        for reach, weight in enumerate(WEIGHTS, start=1):
            total = total + weight * (near[centre - reach] + near[centre + reach])
        totals.append(total)
    return totals


def over_rows(depth, step):
    def body(index, carry):
        step(pl.ds(pl.multiple_of(index * ROWS, ROWS), ROWS), pl.multiple_of(index * ROWS, ROWS))
        return carry

    lax.fori_loop(0, depth // ROWS, body, 0, unroll=2)


def spread_kernel(shots, width_x, me_ref, ax_ref, ay_ref, in_ref, out_ref, near_ref, far_ref):
    width_y = in_ref.shape[1]
    first = me_ref[0] * width_x
    near_ref[...] = jnp.zeros_like(near_ref)
    far_ref[...] = jnp.zeros_like(far_ref)
    lane = lax.broadcasted_iota(jnp.int32, (width_x, width_y), 1)

    def body(shot, carry):
        start = pl.multiple_of(shot * width_x, width_x)
        column = ay_ref[shot]
        moved = pltpu.roll(in_ref[pl.ds(start, width_x), :], lax.rem(column, width_y), 1)
        rows = pl.ds(ax_ref[shot] + first, width_x)
        near_ref[rows, :] = near_ref[rows, :] + jnp.where(lane < column, 0.0, moved)
        far_ref[rows, :] = far_ref[rows, :] + jnp.where(lane < column, moved, 0.0)
        return carry

    lax.fori_loop(0, shots, body, 0, unroll=8)
    out_ref[:, :width_y] = near_ref[...]
    out_ref[:, width_y:] = far_ref[...]


def cell(flat, across, width_y):
    shift_y = width_y.bit_length() - 1
    shift_x = across.bit_length() - 1
    row = lax.shift_right_logical(flat, shift_y)
    return lax.shift_right_logical(row, shift_x), row & (across - 1), flat & (width_y - 1)


def receiver_kernel(count, across, depth, index_ref, seen_ref, out_ref):
    width_y = out_ref.shape[2]
    out_ref[...] = jnp.zeros_like(out_ref)
    shape = out_ref.shape[1:]
    lane = lax.broadcasted_iota(jnp.int32, shape, 1)
    line = lax.broadcasted_iota(jnp.int32, shape, 0)

    def body(receiver, carry):
        cell_z, cell_x, cell_y = cell(index_ref[receiver], across, width_y)
        value = jnp.where(line == 1, seen_ref[0, 0, receiver], 1.0)
        value = jnp.where(line == 2, seen_ref[1, 0, receiver], value)
        value = jnp.where(line == 3, seen_ref[2, 0, receiver], value)
        row = cell_x * depth + cell_z
        out_ref[row] = out_ref[row] + jnp.where(lane == cell_y, value, 0.0)
        return carry

    lax.fori_loop(0, count, body, 0, unroll=4)


def first_kernel(
    shots, depth, width_x, me_ref, ax_ref, ay_ref, model_hbm, before_hbm, now_hbm, later_hbm, latest_hbm,
    fields_hbm, panels_hbm,
    near_ref, far_ref, before_ref, now_ref, later_ref, latest_ref, turn_ref, fields_ref, panels_ref, in_sems, out_sems,
):
    block = depth * width_x
    width_y = panels_ref.shape[1]
    pairs = (
        (now_hbm, now_ref),
        (before_hbm, before_ref),
        (later_hbm, later_ref),
        (latest_hbm, latest_ref),
        (model_hbm.at[:, :width_y], near_ref),
        (model_hbm.at[:, width_y:], far_ref),
    )
    loads = [pltpu.make_async_copy(source, ref, in_sems.at[k]) for k, (source, ref) in enumerate(pairs)]
    for load in loads:
        load.start()

    def put(place, value):
        turn_ref[...] = value
        flat = turn_ref.reshape(block, width_y)
        for row in range(width_x):
            fields_ref[pl.ds(place * block + row * depth, depth), :] = flat[pl.ds(row, depth, stride=width_x), :]

    for load in loads[:4]:
        load.wait()
    now = now_ref[...].astype(jnp.float32)
    put(0, now)
    put(1, 2.0 * now - before_ref[...].astype(jnp.float32))
    later = later_ref[...].astype(jnp.float32)
    put(2, later)
    put(3, 2.0 * later - latest_ref[...].astype(jnp.float32))
    keep_fields = pltpu.make_async_copy(fields_ref, fields_hbm, out_sems.at[0])
    keep_fields.start()
    for load in loads[4:]:
        load.wait()
    first = me_ref[0] * width_x
    lane = lax.broadcasted_iota(jnp.int32, (width_x, width_y), 1)

    def cut(shot, carry):
        rows = pl.ds(ax_ref[shot] + first, width_x)
        column = ay_ref[shot]
        turn = lax.rem(2 * width_y - column, width_y)
        near = pltpu.roll(near_ref[rows, :], turn, 1)
        far = pltpu.roll(far_ref[rows, :], turn, 1)
        start = pl.multiple_of(shot * width_x, width_x)
        panels_ref[pl.ds(start, width_x), :] = jnp.where(lane < width_y - column, near, far)
        return carry

    lax.fori_loop(0, shots, cut, 0, unroll=8)
    keep_panels = pltpu.make_async_copy(panels_ref, panels_hbm, out_sems.at[1])
    keep_panels.start()
    keep_fields.wait()
    keep_panels.wait()


def slab_slice(ref, first, depth, width_x, row):
    return ref[pl.ds(first + row, depth, stride=width_x), :]


def before_kernel(
    slabs, depth, width_x, me_ref, own_ref, left_ref, right_ref, far_a_ref, far_b_ref, band_ref,
    start_ref, push_ref, later_ref, back_ref, curve_ref, part_ref, sems,
):
    me = me_ref[0]
    across = slabs * width_x
    outs = (start_ref, push_ref, later_ref, back_ref)
    copies = []
    for distance, pieces in (
        (0, [(own_ref, k) for k in range(4)]),
        (slabs - 1, [(left_ref, k) for k in range(4)]),
        (1, [(right_ref, k) for k in range(4)]),
        (2, [(far_a_ref, 0), (far_a_ref, 1), (far_b_ref, 0), (far_b_ref, 1)]),
    ):
        base = lax.rem(me + distance, slabs) * width_x
        for field, ((ref, place), out) in enumerate(zip(pieces, outs)):
            offset = REACH if field == 0 else 0
            source = ref.at[pl.ds(place * width_x, width_x)]
            target = out.at[pl.ds(base + offset, width_x)]
            copies.append((field, pltpu.make_async_copy(source, target, sems.at[field])))
    copies.sort(key=lambda item: item[0])
    for _, copy in copies:
        copy.start()
    zeros = jnp.zeros(start_ref.shape[1:], jnp.float32)
    for row in range(REACH):
        start_ref[row] = zeros
        start_ref[REACH + across + row] = zeros
    for field, copy in copies:
        if field == 0:
            copy.wait()

    def curve(slab, carry):
        x = slab * width_x
        along(start_ref, x, width_x, band_ref, part_ref)

        def step(rows, _):
            for index, bend in enumerate(laplace(start_ref, x, width_x, rows, part_ref)):
                curve_ref[x + index, rows, :] = bend

        over_rows(depth, step)
        return carry

    lax.fori_loop(0, slabs, curve, 0)
    for field, copy in copies:
        if field:
            copy.wait()


def main_kernel(
    slabs, depth, width_x, me_ref, source_ref, wave_ref, own_ref, left_ref, right_ref, far_ref,
    start_ref, push_ref, later_ref, back_ref, curve_ref, extra_ref, band_ref,
    grad_ref, first_ref, second_ref,
    speed_ref, one_ref, two_ref, scaled_ref, again_ref, curve_one_ref, lam_ref, lam_two_ref, sum_ref, mark_ref,
    part_ref, other_ref,
):
    me = me_ref[0]
    across = slabs * width_x
    width_y = mark_ref.shape[1]
    for distance, ref in ((0, own_ref), (slabs - 1, left_ref), (1, right_ref), (2, far_ref)):
        base = lax.rem(me + distance, slabs) * width_x
        for row in range(width_x):
            speed_ref[base + row] = slab_slice(ref, 0, depth, width_x, row)
    zeros = jnp.zeros((depth, width_y), jnp.float32)
    for ref in (one_ref, two_ref, scaled_ref, again_ref):
        for row in range(REACH):
            ref[row] = zeros
            ref[REACH + across + row] = zeros
    source_z, source_x, source_y = cell(source_ref[0], across, width_y)
    spot_z = lax.broadcasted_iota(jnp.int32, (depth, width_y), 0) == source_z
    spot_y = lax.broadcasted_iota(jnp.int32, (depth, width_y), 1) == source_y
    mark_ref[...] = jnp.where(spot_z & spot_y, 1.0, 0.0)

    def pulse(x, step, rows):
        return mark_ref[rows, :] * jnp.where(x == source_x, wave_ref[0, step], 0.0)

    def extra(x, line, first):
        return extra_ref[pl.ds((x * depth + first) * 4 + line, ROWS, stride=4), :]

    def by_slabs(step, slices):
        low = jnp.maximum(me - slices // width_x, 0)
        high = jnp.minimum(me + 1 + slices // width_x, slabs)

        def body(slab, carry):
            step(slab * width_x)
            return carry

        lax.fori_loop(low, high, body, 0)

    def step_one(x):
        def step(rows, _):
            for here in range(width_x):
                here = x + here
                speed = speed_ref[here, rows, :]
                one_ref[here + REACH, rows, :] = (
                    push_ref[here, rows, :] + speed * curve_ref[here, rows, :] + pulse(here, 0, rows)
                )
                scaled_ref[here + REACH, rows, :] = speed * later_ref[here, rows, :]

        over_rows(depth, step)

    by_slabs(step_one, across)

    def step_two(x):
        along(one_ref, x, width_x, band_ref, part_ref)

        def step(rows, _):
            for index, bend in enumerate(laplace(one_ref, x, width_x, rows, part_ref)):
                here = x + index
                curve_one_ref[here, rows, :] = bend
                two_ref[here + REACH, rows, :] = (
                    2.0 * one_ref[here + REACH, rows, :]
                    - start_ref[here + REACH, rows, :]
                    + speed_ref[here, rows, :] * bend
                    + pulse(here, 1, rows)
                )

        over_rows(depth, step)

    by_slabs(step_two, across)

    def back_three(x):
        along(two_ref, x, width_x, band_ref, part_ref)
        along(scaled_ref, x, width_x, band_ref, other_ref)

        def step(rows, first):
            bends = laplace(two_ref, x, width_x, rows, part_ref)
            backs = laplace(scaled_ref, x, width_x, rows, other_ref)
            for index, (bend, back) in enumerate(zip(bends, backs)):
                here = x + index
                speed = speed_ref[here, rows, :]
                three = (
                    2.0 * two_ref[here + REACH, rows, :]
                    - one_ref[here + REACH, rows, :]
                    + speed * bend
                    + pulse(here, 2, rows)
                )
                lam = back_ref[here, rows, :] + back
                lam = lam + (extra(here, 0, first) * three - extra(here, 3, first))
                lam_ref[here, rows, :] = lam
                sum_ref[here, rows, :] = lam * bend
                again_ref[here + REACH, rows, :] = speed * lam

        over_rows(depth, step)

    by_slabs(back_three, 2 * REACH)

    def back_two(x):
        along(again_ref, x, width_x, band_ref, part_ref)

        def step(rows, first):
            for index, back in enumerate(laplace(again_ref, x, width_x, rows, part_ref)):
                here = x + index
                lam = 2.0 * lam_ref[here, rows, :] - later_ref[here, rows, :] + back
                lam = lam + (extra(here, 0, first) * two_ref[here + REACH, rows, :] - extra(here, 2, first))
                lam_two_ref[here, rows, :] = lam
                sum_ref[here, rows, :] = sum_ref[here, rows, :] + lam * curve_one_ref[here, rows, :]
                scaled_ref[here + REACH, rows, :] = speed_ref[here, rows, :] * lam

        over_rows(depth, step)

    by_slabs(back_two, REACH)

    x = me * width_x
    along(scaled_ref, x, width_x, band_ref, part_ref)

    def step(rows, first):
        for index, back in enumerate(laplace(scaled_ref, x, width_x, rows, part_ref)):
            here = x + index
            lam_two = lam_two_ref[here, rows, :]
            lam = 2.0 * lam_two - lam_ref[here, rows, :] + back
            lam = lam + (extra(here, 0, first) * one_ref[here + REACH, rows, :] - extra(here, 1, first))
            first_ref[index, rows, :] = lam.astype(first_ref.dtype)
            second_ref[index, rows, :] = lam_two.astype(second_ref.dtype)
            grad_ref[pl.ds(first * width_x + index, ROWS, stride=width_x), :] = (
                sum_ref[here, rows, :] + lam * curve_ref[here, rows, :]
            )

    over_rows(depth, step)


def shift(x, distance):
    count = lax.axis_size("sub")
    return lax.ppermute(x, "sub", [(i, (i + distance) % count) for i in range(count)])


def per_device(
    model,
    anchor_x,
    anchor_y,
    state_before,
    state_now,
    adjoint_later,
    adjoint_latest,
    wavelet,
    src_index,
    rec_index,
    observed,
):
    groups = lax.axis_size("shots")
    slabs = lax.axis_size("sub")
    _, model_x, model_y = model.shape
    depth, width_x, width_y = state_now.shape[1:]
    across = width_x * slabs
    block = depth * width_x
    me = lax.axis_index("sub").astype(jnp.int32)[None]
    weights = band(width_y)
    f32 = jnp.float32

    def shape(*dims):
        return jax.ShapeDtypeStruct(dims, f32)

    state = pltpu.VMEM((depth, width_x, width_y), jnp.bfloat16)
    fields, panels = pl.pallas_call(
        functools.partial(first_kernel, groups, depth, width_x),
        out_shape=[shape(4 * block, width_y), shape(groups * width_x, width_y)],
        in_specs=[SMEM] * 3 + [HBM] * 5,
        out_specs=[HBM] * 2,
        scratch_shapes=[pltpu.VMEM((model_x, width_y), f32)] * 2
        + [state] * 4
        + [
            pltpu.VMEM((depth, width_x, width_y), f32),
            pltpu.VMEM((4 * block, width_y), f32),
            pltpu.VMEM((groups * width_x, width_y), f32),
            pltpu.SemaphoreType.DMA((6,)),
            pltpu.SemaphoreType.DMA((2,)),
        ],
        name="first",
    )(me, anchor_x, anchor_y, model[0], state_before[0], state_now[0], adjoint_later[0], adjoint_latest[0])
    left = shift(fields, 1)
    right = shift(fields, -1)
    far_a = shift(left[: 2 * block], 1)
    far_b = shift(right[2 * block :], -1)

    speed = lax.all_to_all(
        panels.reshape(groups, width_x, width_y), "shots", split_axis=0, concat_axis=0, tiled=True
    ).reshape(block, width_y)

    extra = pl.pallas_call(
        functools.partial(receiver_kernel, rec_index.shape[1], across, depth),
        out_shape=shape(across * depth, 4, width_y),
        in_specs=[SMEM, SMEM],
        out_specs=VMEM,
        compiler_params=PARAMS,
        name="receivers",
    )(rec_index[0], jnp.transpose(observed, (1, 0, 2))).reshape(across * depth * 4, width_y)

    whole = (across, depth, width_y)
    padded = (across + 2 * REACH, depth, width_y)
    start, push, late, back, curve = pl.pallas_call(
        functools.partial(before_kernel, slabs, depth, width_x),
        out_shape=[shape(*padded)] + [shape(*whole)] * 4,
        in_specs=[SMEM] + [HBM] * 5 + [VMEM],
        out_specs=[VMEM] * 5,
        scratch_shapes=[pltpu.VMEM((width_x, depth, width_y), f32), pltpu.SemaphoreType.DMA((4,))],
        compiler_params=PARAMS,
        name="before",
    )(me, *(piece.reshape(-1, depth, width_y) for piece in (fields, left, right, far_a, far_b)), weights)

    speed, extra = lax.optimization_barrier((speed, extra))
    speed_left = shift(speed, 1)
    speed_right = shift(speed, -1)
    speed_far = shift(speed, 2)

    slab = jax.ShapeDtypeStruct((width_x, depth, width_y), jnp.bfloat16)
    grad, first, second = pl.pallas_call(
        functools.partial(main_kernel, slabs, depth, width_x),
        out_shape=[shape(block, width_y), slab, slab],
        in_specs=[SMEM] * 3 + [VMEM] * 11,
        out_specs=[VMEM] * 3,
        scratch_shapes=[
            pltpu.VMEM(whole, f32),
            pltpu.VMEM(padded, f32),
            pltpu.VMEM(padded, f32),
            pltpu.VMEM(padded, f32),
            pltpu.VMEM(padded, f32),
            pltpu.VMEM(whole, f32),
            pltpu.VMEM(whole, f32),
            pltpu.VMEM(whole, f32),
            pltpu.VMEM(whole, f32),
            pltpu.VMEM((depth, width_y), f32),
            pltpu.VMEM((width_x, depth, width_y), f32),
            pltpu.VMEM((width_x, depth, width_y), f32),
        ],
        compiler_params=PARAMS,
        name="window",
    )(
        me, src_index, wavelet, speed, speed_left, speed_right, speed_far,
        start, push, late, back, curve, extra, weights,
    )

    returned = lax.all_to_all(
        grad.reshape(groups, width_x, width_y), "shots", split_axis=0, concat_axis=0, tiled=True
    ).reshape(groups * width_x, width_y)
    owned = pl.pallas_call(
        functools.partial(spread_kernel, groups, width_x),
        out_shape=shape(model_x, model_y),
        in_specs=[SMEM, SMEM, SMEM, VMEM],
        out_specs=VMEM,
        scratch_shapes=[pltpu.VMEM((model_x, width_y), f32)] * 2,
        compiler_params=PARAMS,
        name="spread",
    )(me, anchor_x, anchor_y, returned)
    parts = lax.all_to_all(
        owned.reshape(slabs, model_x // slabs, model_y), "sub", split_axis=0, concat_axis=0, tiled=True
    )
    gradient = parts[0]
    for index in range(1, slabs):
        gradient = gradient + parts[index]
    return (
        gradient[None],
        jnp.transpose(first, (1, 0, 2))[None],
        jnp.transpose(second, (1, 0, 2))[None],
    )


def solution(mesh):
    return jax.shard_map(
        per_device,
        mesh=mesh,
        in_specs=(
            P("shots", None, None),
            P(),
            P(),
            P("shots", None, "sub", None),
            P("shots", None, "sub", None),
            P("shots", None, "sub", None),
            P("shots", None, "sub", None),
            P("shots", None),
            P("shots"),
            P("shots", None),
            P("shots", None, None),
        ),
        out_specs=(
            P("shots", "sub", None),
            P("shots", None, "sub", None),
            P("shots", None, "sub", None),
        ),
        check_vma=False,
    )
```

```python
import functools

import jax
import jax.numpy as jnp
import numpy as np
from jax import lax
from jax.experimental import pallas as pl
from jax.experimental.pallas import tpu as pltpu
from jax.sharding import PartitionSpec as P

STEPS = 3
REACH = 4
UNIT = 5040.0
WHOLE = (8064.0, -1008.0, 128.0, -9.0)
CENTRE = 3.0 * (-205.0 / 72.0)
WEIGHTS = (8.0 / 5.0, -1.0 / 5.0, 8.0 / 315.0, -1.0 / 560.0)

SMEM = pl.BlockSpec(memory_space=pltpu.SMEM)
HBM = pl.BlockSpec(memory_space=pltpu.HBM)
VMEM = pl.BlockSpec(memory_space=pltpu.VMEM)
PARAMS = pltpu.CompilerParams(vmem_limit_bytes=24 << 20)


def band(size):
    offset = np.abs(np.arange(size)[:, None] - np.arange(size)[None, :])
    matrix = np.zeros((size, size), np.float32)
    for reach, weight in enumerate(WHOLE, start=1):
        matrix[offset == reach] = weight
    return jnp.asarray(matrix, jnp.bfloat16)


ROWS = 16
GROUP = 2


def along(ref, x, count, band_ref, part_ref):
    weights = band_ref[...]
    twice_down = jnp.concatenate([weights, weights], axis=0)
    twice_across = jnp.concatenate([weights, weights], axis=1)
    for index in range(0, count, 2):
        highs, lows = [], []
        for slice_x in (x + REACH + index, x + REACH + index + 1):
            centre = ref[slice_x]
            highs.append(centre.astype(jnp.bfloat16))
            lows.append((centre - highs[-1].astype(jnp.float32)).astype(jnp.bfloat16))
        beside = [jnp.concatenate(pair, axis=1) for pair in zip(highs, lows)]
        along_y = jnp.dot(jnp.concatenate(beside, axis=0), twice_down, preferred_element_type=jnp.float32)
        above = jnp.concatenate([jnp.concatenate(highs, axis=1), jnp.concatenate(lows, axis=1)], axis=0)
        along_z = jnp.dot(twice_across, above, preferred_element_type=jnp.float32)
        size = weights.shape[0]
        part_ref[index] = along_y[:size] + along_z[:, :size]
        part_ref[index + 1] = along_y[size:] + along_z[:, size:]


def laplace(ref, x, count, rows, part_ref):
    near = [ref[x + index, rows, :] for index in range(count + 2 * REACH)]
    totals = []
    for index in range(count):
        centre = index + REACH
        total = CENTRE * near[centre] + part_ref[index, rows, :] * (1.0 / UNIT)
        for reach, weight in enumerate(WEIGHTS, start=1):
            total = total + weight * (near[centre - reach] + near[centre + reach])
        totals.append(total)
    return totals


def over_rows(depth, step):
    def body(index, carry):
        step(pl.ds(pl.multiple_of(index * ROWS, ROWS), ROWS), pl.multiple_of(index * ROWS, ROWS))
        return carry

    lax.fori_loop(0, depth // ROWS, body, 0, unroll=8)


def spread_kernel(shots, width_x, me_ref, ax_ref, ay_ref, in_ref, out_ref, near_ref, far_ref):
    width_y = in_ref.shape[1]
    first = me_ref[0] * width_x
    near_ref[...] = jnp.zeros_like(near_ref)
    far_ref[...] = jnp.zeros_like(far_ref)
    lane = lax.broadcasted_iota(jnp.int32, (width_x, width_y), 1)

    def body(shot, carry):
        start = pl.multiple_of(shot * width_x, width_x)
        column = ay_ref[shot]
        moved = pltpu.roll(in_ref[pl.ds(start, width_x), :], lax.rem(column, width_y), 1)
        rows = pl.ds(ax_ref[shot] + first, width_x)
        near_ref[rows, :] = near_ref[rows, :] + jnp.where(lane < column, 0.0, moved)
        far_ref[rows, :] = far_ref[rows, :] + jnp.where(lane < column, moved, 0.0)
        return carry

    lax.fori_loop(0, shots, body, 0, unroll=8)
    out_ref[:, :width_y] = near_ref[...]
    out_ref[:, width_y:] = far_ref[...]


def cell(flat, across, width_y):
    shift_y = width_y.bit_length() - 1
    shift_x = across.bit_length() - 1
    row = lax.shift_right_logical(flat, shift_y)
    return lax.shift_right_logical(row, shift_x), row & (across - 1), flat & (width_y - 1)


def receiver_kernel(count, across, depth, index_hbm, seen_hbm, out_ref, index_ref, seen_ref, sems):
    width_y = out_ref.shape[1]
    load_index = pltpu.make_async_copy(index_hbm, index_ref, sems.at[0])
    load_seen = pltpu.make_async_copy(seen_hbm, seen_ref, sems.at[1])
    load_index.start()
    load_seen.start()
    out_ref[...] = jnp.zeros_like(out_ref)
    load_index.wait()
    load_seen.wait()
    shape = (4, width_y)
    lane = lax.broadcasted_iota(jnp.int32, shape, 1)
    line = lax.broadcasted_iota(jnp.int32, shape, 0)

    def body(group, carry):
        starts, sums = [], []
        for member in range(GROUP):
            receiver = group * GROUP + member
            cell_z, cell_x, cell_y = cell(index_ref[0, receiver], across, width_y)
            value = jnp.where(line == 1, seen_ref[0, 0, receiver], 1.0)
            value = jnp.where(line == 2, seen_ref[1, 0, receiver], value)
            value = jnp.where(line == 3, seen_ref[2, 0, receiver], value)
            start = pl.multiple_of((cell_x * depth + cell_z) * 4, 4)
            tile = out_ref[pl.ds(start, 4), :]
            for earlier, total in zip(starts, sums):
                tile = jnp.where(earlier == start, total, tile)
            starts.append(start)
            sums.append(tile + jnp.where(lane == cell_y, value, 0.0))
        for start, total in zip(starts, sums):
            out_ref[pl.ds(start, 4), :] = total
        return carry

    lax.fori_loop(0, count // GROUP, body, 0, unroll=4)


def first_kernel(
    shots, depth, width_x, me_ref, ax_hbm, ay_hbm, model_hbm, before_hbm, now_hbm, later_hbm, latest_hbm,
    fields_hbm, panels_hbm,
    near_ref, far_ref, before_ref, now_ref, later_ref, latest_ref, turn_ref, fields_ref, panels_ref, ax_ref, ay_ref, in_sems, out_sems,
):
    block = depth * width_x
    width_y = panels_ref.shape[1]
    pairs = (
        (now_hbm, now_ref),
        (before_hbm, before_ref),
        (later_hbm, later_ref),
        (latest_hbm, latest_ref),
        (model_hbm.at[:, :width_y], near_ref),
        (model_hbm.at[:, width_y:], far_ref),
        (ax_hbm, ax_ref),
        (ay_hbm, ay_ref),
    )
    loads = [pltpu.make_async_copy(source, ref, in_sems.at[k]) for k, (source, ref) in enumerate(pairs)]
    for load in loads:
        load.start()

    def put(place, value):
        turn_ref[...] = value
        flat = turn_ref.reshape(block, width_y)
        for row in range(width_x):
            fields_ref[pl.ds(place * block + row * depth, depth), :] = flat[pl.ds(row, depth, stride=width_x), :]

    for load in loads[:4]:
        load.wait()
    now = now_ref[...].astype(jnp.float32)
    put(0, now)
    put(1, 2.0 * now - before_ref[...].astype(jnp.float32))
    later = later_ref[...].astype(jnp.float32)
    put(2, later)
    put(3, 2.0 * later - latest_ref[...].astype(jnp.float32))
    keep_fields = pltpu.make_async_copy(fields_ref, fields_hbm, out_sems.at[0])
    keep_fields.start()
    for load in loads[4:]:
        load.wait()
    first = me_ref[0] * width_x
    lane = lax.broadcasted_iota(jnp.int32, (width_x, width_y), 1)

    def cut(shot, carry):
        rows = pl.ds(ax_ref[shot] + first, width_x)
        column = ay_ref[shot]
        turn = lax.rem(2 * width_y - column, width_y)
        near = pltpu.roll(near_ref[rows, :], turn, 1)
        far = pltpu.roll(far_ref[rows, :], turn, 1)
        start = pl.multiple_of(shot * width_x, width_x)
        panels_ref[pl.ds(start, width_x), :] = jnp.where(lane < width_y - column, near, far)
        return carry

    lax.fori_loop(0, shots, cut, 0, unroll=8)
    keep_panels = pltpu.make_async_copy(panels_ref, panels_hbm, out_sems.at[1])
    keep_panels.start()
    keep_fields.wait()
    keep_panels.wait()


def slab_slice(ref, first, depth, width_x, row):
    return ref[pl.ds(first + row, depth, stride=width_x), :]


def before_kernel(
    slabs, depth, width_x, me_ref, own_ref, left_ref, right_ref, far_a_ref, far_b_ref, band_ref,
    start_ref, push_ref, later_ref, back_ref, curve_ref, part_ref, sems,
):
    me = me_ref[0]
    across = slabs * width_x
    outs = (start_ref, push_ref, later_ref, back_ref)
    copies = []
    for distance, pieces in (
        (0, [(own_ref, k) for k in range(4)]),
        (slabs - 1, [(left_ref, k) for k in range(4)]),
        (1, [(right_ref, k) for k in range(4)]),
        (2, [(far_a_ref, 0), (far_a_ref, 1), (far_b_ref, 0), (far_b_ref, 1)]),
    ):
        base = lax.rem(me + distance, slabs) * width_x
        for field, ((ref, place), out) in enumerate(zip(pieces, outs)):
            offset = REACH if field == 0 else 0
            source = ref.at[pl.ds(place * width_x, width_x)]
            target = out.at[pl.ds(base + offset, width_x)]
            copies.append((field, pltpu.make_async_copy(source, target, sems.at[field])))
    copies.sort(key=lambda item: item[0])
    for _, copy in copies:
        copy.start()
    zeros = jnp.zeros(start_ref.shape[1:], jnp.float32)
    for row in range(REACH):
        start_ref[row] = zeros
        start_ref[REACH + across + row] = zeros
    for field, copy in copies:
        if field == 0:
            copy.wait()

    def curve(slab, carry):
        x = slab * width_x
        along(start_ref, x, width_x, band_ref, part_ref)

        def step(rows, _):
            for index, bend in enumerate(laplace(start_ref, x, width_x, rows, part_ref)):
                curve_ref[x + index, rows, :] = bend

        over_rows(depth, step)
        return carry

    lax.fori_loop(0, slabs, curve, 0)
    for field, copy in copies:
        if field:
            copy.wait()


def main_kernel(
    slabs, depth, width_x, me_ref, source_ref, wave_ref, own_ref, left_ref, right_ref, far_ref,
    start_ref, push_ref, later_ref, back_ref, curve_ref, extra_hbm, band_ref,
    grad_ref, first_ref, second_ref,
    speed_ref, one_ref, two_ref, scaled_ref, again_ref, curve_one_ref, lam_ref, lam_two_ref, sum_ref, mark_ref,
    part_ref, other_ref, extra_ref, extra_sem,
):
    me = me_ref[0]
    across = slabs * width_x
    width_y = mark_ref.shape[1]
    load_extra = pltpu.make_async_copy(extra_hbm, extra_ref, extra_sem)
    load_extra.start()
    for distance, ref in ((0, own_ref), (slabs - 1, left_ref), (1, right_ref), (2, far_ref)):
        base = lax.rem(me + distance, slabs) * width_x
        for row in range(width_x):
            speed_ref[base + row] = slab_slice(ref, 0, depth, width_x, row)
    zeros = jnp.zeros((depth, width_y), jnp.float32)
    for ref in (one_ref, two_ref, scaled_ref, again_ref):
        for row in range(REACH):
            ref[row] = zeros
            ref[REACH + across + row] = zeros
    source_z, source_x, source_y = cell(source_ref[0], across, width_y)
    spot_z = lax.broadcasted_iota(jnp.int32, (depth, width_y), 0) == source_z
    spot_y = lax.broadcasted_iota(jnp.int32, (depth, width_y), 1) == source_y
    mark_ref[...] = jnp.where(spot_z & spot_y, 1.0, 0.0)

    def add_source(ref, step):
        row = pl.ds(source_z, 1)
        lane = lax.broadcasted_iota(jnp.int32, (1, width_y), 1)
        pulse = jnp.where(lane == source_y, wave_ref[0, step], 0.0)
        ref[source_x + REACH, row, :] = ref[source_x + REACH, row, :] + pulse

    def pulse(x, step, rows):
        return mark_ref[rows, :] * jnp.where(x == source_x, wave_ref[0, step], 0.0)

    def extra(x, line, first):
        return extra_ref[pl.ds((x * depth + first) * 4 + line, ROWS, stride=4), :]

    def by_slabs(step, slices):
        low = jnp.maximum(me - slices // width_x, 0)
        high = jnp.minimum(me + 1 + slices // width_x, slabs)

        def body(slab, carry):
            step(slab * width_x)
            return carry

        lax.fori_loop(low, high, body, 0)

    def step_one(x):
        def step(rows, _):
            for here in range(width_x):
                here = x + here
                speed = speed_ref[here, rows, :]
                one_ref[here + REACH, rows, :] = (
                    push_ref[here, rows, :] + speed * curve_ref[here, rows, :]
                )
                scaled_ref[here + REACH, rows, :] = speed * later_ref[here, rows, :]

        over_rows(depth, step)

    by_slabs(step_one, across)
    add_source(one_ref, 0)

    def step_two(x):
        along(one_ref, x, width_x, band_ref, part_ref)

        def step(rows, _):
            for index, bend in enumerate(laplace(one_ref, x, width_x, rows, part_ref)):
                here = x + index
                curve_one_ref[here, rows, :] = bend
                two_ref[here + REACH, rows, :] = (
                    2.0 * one_ref[here + REACH, rows, :]
                    - start_ref[here + REACH, rows, :]
                    + speed_ref[here, rows, :] * bend
                )

        over_rows(depth, step)

    by_slabs(step_two, across)
    add_source(two_ref, 1)

    def back_three(x):
        along(two_ref, x, width_x, band_ref, part_ref)
        along(scaled_ref, x, width_x, band_ref, other_ref)

        def step(rows, first):
            bends = laplace(two_ref, x, width_x, rows, part_ref)
            backs = laplace(scaled_ref, x, width_x, rows, other_ref)
            for index, (bend, back) in enumerate(zip(bends, backs)):
                here = x + index
                speed = speed_ref[here, rows, :]
                three = (
                    2.0 * two_ref[here + REACH, rows, :]
                    - one_ref[here + REACH, rows, :]
                    + speed * bend
                    + pulse(here, 2, rows)
                )
                lam = back_ref[here, rows, :] + back
                lam = lam + (extra(here, 0, first) * three - extra(here, 3, first))
                lam_ref[here, rows, :] = lam
                sum_ref[here, rows, :] = lam * bend
                again_ref[here + REACH, rows, :] = speed * lam

        over_rows(depth, step)

    load_extra.wait()
    by_slabs(back_three, 2 * REACH)

    def back_two(x):
        along(again_ref, x, width_x, band_ref, part_ref)

        def step(rows, first):
            for index, back in enumerate(laplace(again_ref, x, width_x, rows, part_ref)):
                here = x + index
                lam = 2.0 * lam_ref[here, rows, :] - later_ref[here, rows, :] + back
                lam = lam + (extra(here, 0, first) * two_ref[here + REACH, rows, :] - extra(here, 2, first))
                lam_two_ref[here, rows, :] = lam
                sum_ref[here, rows, :] = sum_ref[here, rows, :] + lam * curve_one_ref[here, rows, :]
                scaled_ref[here + REACH, rows, :] = speed_ref[here, rows, :] * lam

        over_rows(depth, step)

    by_slabs(back_two, REACH)

    x = me * width_x
    along(scaled_ref, x, width_x, band_ref, part_ref)

    def step(rows, first):
        for index, back in enumerate(laplace(scaled_ref, x, width_x, rows, part_ref)):
            here = x + index
            lam_two = lam_two_ref[here, rows, :]
            lam = 2.0 * lam_two - lam_ref[here, rows, :] + back
            lam = lam + (extra(here, 0, first) * one_ref[here + REACH, rows, :] - extra(here, 1, first))
            first_ref[index, rows, :] = lam.astype(first_ref.dtype)
            second_ref[index, rows, :] = lam_two.astype(second_ref.dtype)
            grad_ref[pl.ds(first * width_x + index, ROWS, stride=width_x), :] = (
                sum_ref[here, rows, :] + lam * curve_ref[here, rows, :]
            )

    over_rows(depth, step)


def shift(x, distance):
    count = lax.axis_size("sub")
    return lax.ppermute(x, "sub", [(i, (i + distance) % count) for i in range(count)])


def per_device(
    model,
    anchor_x,
    anchor_y,
    state_before,
    state_now,
    adjoint_later,
    adjoint_latest,
    wavelet,
    src_index,
    rec_index,
    observed,
):
    groups = lax.axis_size("shots")
    slabs = lax.axis_size("sub")
    _, model_x, model_y = model.shape
    depth, width_x, width_y = state_now.shape[1:]
    across = width_x * slabs
    block = depth * width_x
    me = lax.axis_index("sub").astype(jnp.int32)[None]
    weights = band(width_y)
    f32 = jnp.float32

    def shape(*dims):
        return jax.ShapeDtypeStruct(dims, f32)

    state = pltpu.VMEM((depth, width_x, width_y), jnp.bfloat16)
    fields, panels = pl.pallas_call(
        functools.partial(first_kernel, groups, depth, width_x),
        out_shape=[shape(4 * block, width_y), shape(groups * width_x, width_y)],
        in_specs=[SMEM] + [HBM] * 7,
        out_specs=[HBM] * 2,
        scratch_shapes=[pltpu.VMEM((model_x, width_y), f32)] * 2
        + [state] * 4
        + [
            pltpu.VMEM((depth, width_x, width_y), f32),
            pltpu.VMEM((4 * block, width_y), f32),
            pltpu.VMEM((groups * width_x, width_y), f32),
            pltpu.SMEM((groups,), jnp.int32),
            pltpu.SMEM((groups,), jnp.int32),
            pltpu.SemaphoreType.DMA((8,)),
            pltpu.SemaphoreType.DMA((2,)),
        ],
        name="first",
    )(me, anchor_x, anchor_y, model[0], state_before[0], state_now[0], adjoint_later[0], adjoint_latest[0])
    left = shift(fields, 1)
    right = shift(fields, -1)
    extra = pl.pallas_call(
        functools.partial(receiver_kernel, rec_index.shape[1], across, depth),
        out_shape=shape(across * depth * 4, width_y),
        in_specs=[HBM, HBM],
        out_specs=VMEM,
        scratch_shapes=[
            pltpu.SMEM((1, rec_index.shape[1]), jnp.int32),
            pltpu.SMEM((STEPS, 1, rec_index.shape[1]), f32),
            pltpu.SemaphoreType.DMA((2,)),
        ],
        name="receivers",
    )(rec_index, jnp.transpose(observed, (1, 0, 2)))

    far_a = shift(left[: 2 * block], 1)
    far_b = shift(right[2 * block :], -1)

    speed = lax.all_to_all(
        panels.reshape(groups, width_x, width_y), "shots", split_axis=0, concat_axis=0, tiled=True
    ).reshape(block, width_y)

    whole = (across, depth, width_y)
    padded = (across + 2 * REACH, depth, width_y)
    start, push, late, back, curve = pl.pallas_call(
        functools.partial(before_kernel, slabs, depth, width_x),
        out_shape=[shape(*padded)] + [shape(*whole)] * 4,
        in_specs=[SMEM] + [HBM] * 5 + [VMEM],
        out_specs=[VMEM] * 5,
        scratch_shapes=[pltpu.VMEM((width_x, depth, width_y), f32), pltpu.SemaphoreType.DMA((4,))],
        compiler_params=PARAMS,
        name="before",
    )(me, *(piece.reshape(-1, depth, width_y) for piece in (fields, left, right, far_a, far_b)), weights)

    speed_far = shift(speed, 2)
    speed_right = shift(speed, -1)
    speed_left = shift(speed, 1)

    slab = jax.ShapeDtypeStruct((width_x, depth, width_y), jnp.bfloat16)
    grad, first, second = pl.pallas_call(
        functools.partial(main_kernel, slabs, depth, width_x),
        out_shape=[shape(block, width_y), slab, slab],
        in_specs=[SMEM] * 3 + [VMEM] * 9 + [HBM, VMEM],
        out_specs=[VMEM] * 3,
        scratch_shapes=[
            pltpu.VMEM(whole, f32),
            pltpu.VMEM(padded, f32),
            pltpu.VMEM(padded, f32),
            pltpu.VMEM(padded, f32),
            pltpu.VMEM(padded, f32),
            pltpu.VMEM(whole, f32),
            pltpu.VMEM(whole, f32),
            pltpu.VMEM(whole, f32),
            pltpu.VMEM(whole, f32),
            pltpu.VMEM((depth, width_y), f32),
            pltpu.VMEM((width_x, depth, width_y), f32),
            pltpu.VMEM((width_x, depth, width_y), f32),
            pltpu.VMEM((across * depth * 4, width_y), f32),
            pltpu.SemaphoreType.DMA,
        ],
        compiler_params=PARAMS,
        name="window",
    )(
        me, src_index, wavelet, speed, speed_left, speed_right, speed_far,
        start, push, late, back, curve, extra, weights,
    )

    returned = lax.all_to_all(
        grad.reshape(groups, width_x, width_y), "shots", split_axis=0, concat_axis=0, tiled=True
    ).reshape(groups * width_x, width_y)
    owned = pl.pallas_call(
        functools.partial(spread_kernel, groups, width_x),
        out_shape=shape(model_x, model_y),
        in_specs=[SMEM, SMEM, SMEM, VMEM],
        out_specs=VMEM,
        scratch_shapes=[pltpu.VMEM((model_x, width_y), f32)] * 2,
        compiler_params=PARAMS,
        name="spread",
    )(me, anchor_x, anchor_y, returned)
    parts = lax.all_to_all(
        owned.reshape(slabs, model_x // slabs, model_y), "sub", split_axis=0, concat_axis=0, tiled=True
    )
    gradient = parts[0]
    for index in range(1, slabs):
        gradient = gradient + parts[index]
    return (
        gradient[None],
        jnp.transpose(first, (1, 0, 2))[None],
        jnp.transpose(second, (1, 0, 2))[None],
    )


def solution(mesh):
    return jax.shard_map(
        per_device,
        mesh=mesh,
        in_specs=(
            P("shots", None, None),
            P(),
            P(),
            P("shots", None, "sub", None),
            P("shots", None, "sub", None),
            P("shots", None, "sub", None),
            P("shots", None, "sub", None),
            P("shots", None),
            P("shots"),
            P("shots", None),
            P("shots", None, None),
        ),
        out_specs=(
            P("shots", "sub", None),
            P("shots", None, "sub", None),
            P("shots", None, "sub", None),
        ),
        check_vma=False,
    )
```

```python
import functools

import jax
import jax.numpy as jnp
import numpy as np
from jax import lax
from jax.experimental import pallas as pl
from jax.experimental.pallas import tpu as pltpu
from jax.sharding import PartitionSpec as P

STEPS = 3
REACH = 4
UNIT = 5040.0
WHOLE = (8064.0, -1008.0, 128.0, -9.0)
CENTRE = 3.0 * (-205.0 / 72.0)
WEIGHTS = (8.0 / 5.0, -1.0 / 5.0, 8.0 / 315.0, -1.0 / 560.0)

SMEM = pl.BlockSpec(memory_space=pltpu.SMEM)
HBM = pl.BlockSpec(memory_space=pltpu.HBM)
VMEM = pl.BlockSpec(memory_space=pltpu.VMEM)
PARAMS = pltpu.CompilerParams(vmem_limit_bytes=24 << 20)


def band(size):
    offset = np.abs(np.arange(size)[:, None] - np.arange(size)[None, :])
    matrix = np.zeros((size, size), np.float32)
    for reach, weight in enumerate(WHOLE, start=1):
        matrix[offset == reach] = weight
    return jnp.asarray(matrix, jnp.bfloat16)


ROWS = 16
GROUP = 2


def along(ref, x, count, band_ref, part_ref):
    weights = band_ref[...]
    twice_down = jnp.concatenate([weights, weights], axis=0)
    twice_across = jnp.concatenate([weights, weights], axis=1)
    for index in range(0, count, 2):
        highs, lows = [], []
        for slice_x in (x + REACH + index, x + REACH + index + 1):
            centre = ref[slice_x]
            highs.append(centre.astype(jnp.bfloat16))
            lows.append((centre - highs[-1].astype(jnp.float32)).astype(jnp.bfloat16))
        beside = [jnp.concatenate(pair, axis=1) for pair in zip(highs, lows)]
        along_y = jnp.dot(jnp.concatenate(beside, axis=0), twice_down, preferred_element_type=jnp.float32)
        above = jnp.concatenate([jnp.concatenate(highs, axis=1), jnp.concatenate(lows, axis=1)], axis=0)
        along_z = jnp.dot(twice_across, above, preferred_element_type=jnp.float32)
        size = weights.shape[0]
        part_ref[index] = along_y[:size] + along_z[:, :size]
        part_ref[index + 1] = along_y[size:] + along_z[:, size:]


def laplace(ref, x, count, rows, part_ref):
    near = [ref[x + index, rows, :] for index in range(count + 2 * REACH)]
    totals = []
    for index in range(count):
        centre = index + REACH
        total = CENTRE * near[centre] + part_ref[index, rows, :] * (1.0 / UNIT)
        for reach, weight in enumerate(WEIGHTS, start=1):
            total = total + weight * (near[centre - reach] + near[centre + reach])
        totals.append(total)
    return totals


def over_rows(depth, step):
    def body(index, carry):
        step(pl.ds(pl.multiple_of(index * ROWS, ROWS), ROWS), pl.multiple_of(index * ROWS, ROWS))
        return carry

    lax.fori_loop(0, depth // ROWS, body, 0, unroll=8)


def spread_kernel(shots, width_x, me_ref, ax_ref, ay_ref, in_ref, out_ref, *sum_refs):
    width_y = in_ref.shape[1]
    first = me_ref[0] * width_x
    for ref in sum_refs:
        ref[...] = jnp.zeros_like(ref)
    lane = lax.broadcasted_iota(jnp.int32, (width_x, width_y), 1)
    pairs = [sum_refs[index : index + 2] for index in range(0, len(sum_refs), 2)]

    def body(group, carry):
        for member, (near_ref, far_ref) in enumerate(pairs):
            shot = group * len(pairs) + member
            start = pl.multiple_of(shot * width_x, width_x)
            column = ay_ref[shot]
            moved = pltpu.roll(in_ref[pl.ds(start, width_x), :], lax.rem(column, width_y), 1)
            rows = pl.ds(ax_ref[shot] + first, width_x)
            near_ref[rows, :] = near_ref[rows, :] + jnp.where(lane < column, 0.0, moved)
            far_ref[rows, :] = far_ref[rows, :] + jnp.where(lane < column, moved, 0.0)
        return carry

    lax.fori_loop(0, shots // len(pairs), body, 0, unroll=16)
    out_ref[:, :width_y] = sum(ref[...] for ref, _ in pairs)
    out_ref[:, width_y:] = sum(ref[...] for _, ref in pairs)


def cell(flat, across, width_y):
    shift_y = width_y.bit_length() - 1
    shift_x = across.bit_length() - 1
    row = lax.shift_right_logical(flat, shift_y)
    return lax.shift_right_logical(row, shift_x), row & (across - 1), flat & (width_y - 1)


def receiver_kernel(count, across, depth, index_hbm, seen_hbm, out_ref, index_ref, seen_ref, sems):
    width_y = out_ref.shape[1]
    load_index = pltpu.make_async_copy(index_hbm, index_ref, sems.at[0])
    load_seen = pltpu.make_async_copy(seen_hbm, seen_ref, sems.at[1])
    load_index.start()
    load_seen.start()
    out_ref[...] = jnp.zeros_like(out_ref)
    load_index.wait()
    load_seen.wait()
    shape = (4, width_y)
    lane = lax.broadcasted_iota(jnp.int32, shape, 1)
    line = lax.broadcasted_iota(jnp.int32, shape, 0)

    def body(group, carry):
        starts, sums = [], []
        for member in range(GROUP):
            receiver = group * GROUP + member
            cell_z, cell_x, cell_y = cell(index_ref[0, receiver], across, width_y)
            value = jnp.where(line == 1, seen_ref[0, 0, receiver], 1.0)
            value = jnp.where(line == 2, seen_ref[1, 0, receiver], value)
            value = jnp.where(line == 3, seen_ref[2, 0, receiver], value)
            start = pl.multiple_of((cell_x * depth + cell_z) * 4, 4)
            tile = out_ref[pl.ds(start, 4), :]
            for earlier, total in zip(starts, sums):
                tile = jnp.where(earlier == start, total, tile)
            starts.append(start)
            sums.append(tile + jnp.where(lane == cell_y, value, 0.0))
        for start, total in zip(starts, sums):
            out_ref[pl.ds(start, 4), :] = total
        return carry

    lax.fori_loop(0, count // GROUP, body, 0, unroll=16)


def first_kernel(
    shots, depth, width_x, me_ref, ax_hbm, ay_hbm, model_hbm, before_hbm, now_hbm, later_hbm, latest_hbm,
    fields_hbm, panels_hbm,
    near_ref, far_ref, before_ref, now_ref, later_ref, latest_ref, turn_ref, fields_ref, panels_ref, ax_ref, ay_ref, in_sems, out_sems,
):
    block = depth * width_x
    width_y = panels_ref.shape[1]
    pairs = (
        (now_hbm, now_ref),
        (before_hbm, before_ref),
        (later_hbm, later_ref),
        (latest_hbm, latest_ref),
        (model_hbm.at[:, :width_y], near_ref),
        (model_hbm.at[:, width_y:], far_ref),
        (ax_hbm, ax_ref),
        (ay_hbm, ay_ref),
    )
    loads = [pltpu.make_async_copy(source, ref, in_sems.at[k]) for k, (source, ref) in enumerate(pairs)]
    for load in loads:
        load.start()

    def put(place, value):
        turn_ref[...] = value
        flat = turn_ref.reshape(block, width_y)
        for row in range(width_x):
            fields_ref[pl.ds(place * block + row * depth, depth), :] = flat[pl.ds(row, depth, stride=width_x), :]

    for load in loads[:4]:
        load.wait()
    now = now_ref[...].astype(jnp.float32)
    put(0, now)
    put(1, 2.0 * now - before_ref[...].astype(jnp.float32))
    later = later_ref[...].astype(jnp.float32)
    put(2, later)
    put(3, 2.0 * later - latest_ref[...].astype(jnp.float32))
    keep_fields = pltpu.make_async_copy(fields_ref, fields_hbm, out_sems.at[0])
    keep_fields.start()
    for load in loads[4:]:
        load.wait()
    first = me_ref[0] * width_x
    lane = lax.broadcasted_iota(jnp.int32, (width_x, width_y), 1)

    def cut(shot, carry):
        rows = pl.ds(ax_ref[shot] + first, width_x)
        column = ay_ref[shot]
        turn = lax.rem(2 * width_y - column, width_y)
        near = pltpu.roll(near_ref[rows, :], turn, 1)
        far = pltpu.roll(far_ref[rows, :], turn, 1)
        start = pl.multiple_of(shot * width_x, width_x)
        panels_ref[pl.ds(start, width_x), :] = jnp.where(lane < width_y - column, near, far)
        return carry

    lax.fori_loop(0, shots, cut, 0, unroll=128)
    keep_panels = pltpu.make_async_copy(panels_ref, panels_hbm, out_sems.at[1])
    keep_panels.start()
    keep_fields.wait()
    keep_panels.wait()


def slab_slice(ref, first, depth, width_x, row):
    return ref[pl.ds(first + row, depth, stride=width_x), :]


def before_kernel(
    slabs, depth, width_x, me_ref, own_ref, left_ref, right_ref, far_a_ref, far_b_ref, band_ref,
    start_ref, push_ref, later_ref, back_ref, curve_ref, part_ref, sems,
):
    me = me_ref[0]
    across = slabs * width_x
    outs = (start_ref, push_ref, later_ref, back_ref)
    copies = []
    for distance, pieces in (
        (0, [(own_ref, k) for k in range(4)]),
        (slabs - 1, [(left_ref, k) for k in range(4)]),
        (1, [(right_ref, k) for k in range(4)]),
        (2, [(far_a_ref, 0), (far_a_ref, 1), (far_b_ref, 0), (far_b_ref, 1)]),
    ):
        base = lax.rem(me + distance, slabs) * width_x
        for field, ((ref, place), out) in enumerate(zip(pieces, outs)):
            offset = REACH if field == 0 else 0
            source = ref.at[pl.ds(place * width_x, width_x)]
            target = out.at[pl.ds(base + offset, width_x)]
            copies.append((field, pltpu.make_async_copy(source, target, sems.at[field])))
    copies.sort(key=lambda item: item[0])
    for _, copy in copies:
        copy.start()
    zeros = jnp.zeros(start_ref.shape[1:], jnp.float32)
    for row in range(REACH):
        start_ref[row] = zeros
        start_ref[REACH + across + row] = zeros
    for field, copy in copies:
        if field == 0:
            copy.wait()

    def curve(slab, carry):
        x = slab * width_x
        along(start_ref, x, width_x, band_ref, part_ref)

        def step(rows, _):
            for index, bend in enumerate(laplace(start_ref, x, width_x, rows, part_ref)):
                curve_ref[x + index, rows, :] = bend

        over_rows(depth, step)
        return carry

    lax.fori_loop(0, slabs, curve, 0)
    for field, copy in copies:
        if field:
            copy.wait()


def main_kernel(
    slabs, depth, width_x, me_ref, source_ref, wave_ref, own_ref, left_ref, right_ref, far_ref,
    start_ref, push_ref, later_ref, back_ref, curve_ref, extra_hbm, band_ref,
    grad_ref, first_ref, second_ref,
    speed_ref, one_ref, two_ref, scaled_ref, again_ref, curve_one_ref, lam_ref, lam_two_ref, sum_ref, mark_ref,
    part_ref, other_ref, extra_ref, extra_sem,
):
    me = me_ref[0]
    across = slabs * width_x
    width_y = mark_ref.shape[1]
    load_extra = pltpu.make_async_copy(extra_hbm, extra_ref, extra_sem)
    load_extra.start()
    for distance, ref in ((0, own_ref), (slabs - 1, left_ref), (1, right_ref), (2, far_ref)):
        base = lax.rem(me + distance, slabs) * width_x
        for row in range(width_x):
            speed_ref[base + row] = slab_slice(ref, 0, depth, width_x, row)
    zeros = jnp.zeros((depth, width_y), jnp.float32)
    for ref in (one_ref, two_ref, scaled_ref, again_ref):
        for row in range(REACH):
            ref[row] = zeros
            ref[REACH + across + row] = zeros
    source_z, source_x, source_y = cell(source_ref[0], across, width_y)
    spot_z = lax.broadcasted_iota(jnp.int32, (depth, width_y), 0) == source_z
    spot_y = lax.broadcasted_iota(jnp.int32, (depth, width_y), 1) == source_y
    mark_ref[...] = jnp.where(spot_z & spot_y, 1.0, 0.0)

    def add_source(ref, step):
        row = pl.ds(source_z, 1)
        lane = lax.broadcasted_iota(jnp.int32, (1, width_y), 1)
        pulse = jnp.where(lane == source_y, wave_ref[0, step], 0.0)
        ref[source_x + REACH, row, :] = ref[source_x + REACH, row, :] + pulse

    def pulse(x, step, rows):
        return mark_ref[rows, :] * jnp.where(x == source_x, wave_ref[0, step], 0.0)

    def extra(x, line, first):
        return extra_ref[pl.ds((x * depth + first) * 4 + line, ROWS, stride=4), :]

    def by_slabs(step, slices):
        low = jnp.maximum(me - slices // width_x, 0)
        high = jnp.minimum(me + 1 + slices // width_x, slabs)

        def body(slab, carry):
            step(slab * width_x)
            return carry

        lax.fori_loop(low, high, body, 0)

    def step_one(x):
        def step(rows, _):
            for here in range(width_x):
                here = x + here
                speed = speed_ref[here, rows, :]
                one_ref[here + REACH, rows, :] = (
                    push_ref[here, rows, :] + speed * curve_ref[here, rows, :]
                )
                scaled_ref[here + REACH, rows, :] = speed * later_ref[here, rows, :]

        over_rows(depth, step)

    for slab in range(slabs):
        step_one(slab * width_x)
    add_source(one_ref, 0)

    def step_two(x):
        part = part_ref if x // width_x % 2 else other_ref
        along(one_ref, x, width_x, band_ref, part)

        def step(rows, _):
            for index, bend in enumerate(laplace(one_ref, x, width_x, rows, part)):
                here = x + index
                curve_one_ref[here, rows, :] = bend
                two_ref[here + REACH, rows, :] = (
                    2.0 * one_ref[here + REACH, rows, :]
                    - start_ref[here + REACH, rows, :]
                    + speed_ref[here, rows, :] * bend
                )

        over_rows(depth, step)

    for slab in range(slabs):
        step_two(slab * width_x)
    add_source(two_ref, 1)

    def back_three(x):
        along(two_ref, x, width_x, band_ref, part_ref)
        along(scaled_ref, x, width_x, band_ref, other_ref)

        def step(rows, first):
            bends = laplace(two_ref, x, width_x, rows, part_ref)
            backs = laplace(scaled_ref, x, width_x, rows, other_ref)
            for index, (bend, back) in enumerate(zip(bends, backs)):
                here = x + index
                speed = speed_ref[here, rows, :]
                three = (
                    2.0 * two_ref[here + REACH, rows, :]
                    - one_ref[here + REACH, rows, :]
                    + speed * bend
                    + pulse(here, 2, rows)
                )
                lam = back_ref[here, rows, :] + back
                lam = lam + (extra(here, 0, first) * three - extra(here, 3, first))
                lam_ref[here, rows, :] = lam
                sum_ref[here, rows, :] = lam * bend
                again_ref[here + REACH, rows, :] = speed * lam

        over_rows(depth, step)

    load_extra.wait()
    by_slabs(back_three, 2 * REACH)

    def back_two(x):
        along(again_ref, x, width_x, band_ref, part_ref)

        def step(rows, first):
            for index, back in enumerate(laplace(again_ref, x, width_x, rows, part_ref)):
                here = x + index
                lam = 2.0 * lam_ref[here, rows, :] - later_ref[here, rows, :] + back
                lam = lam + (extra(here, 0, first) * two_ref[here + REACH, rows, :] - extra(here, 2, first))
                lam_two_ref[here, rows, :] = lam
                sum_ref[here, rows, :] = sum_ref[here, rows, :] + lam * curve_one_ref[here, rows, :]
                scaled_ref[here + REACH, rows, :] = speed_ref[here, rows, :] * lam

        over_rows(depth, step)

    by_slabs(back_two, REACH)

    x = me * width_x
    along(scaled_ref, x, width_x, band_ref, part_ref)

    def step(rows, first):
        for index, back in enumerate(laplace(scaled_ref, x, width_x, rows, part_ref)):
            here = x + index
            lam_two = lam_two_ref[here, rows, :]
            lam = 2.0 * lam_two - lam_ref[here, rows, :] + back
            lam = lam + (extra(here, 0, first) * one_ref[here + REACH, rows, :] - extra(here, 1, first))
            first_ref[index, rows, :] = lam.astype(first_ref.dtype)
            second_ref[index, rows, :] = lam_two.astype(second_ref.dtype)
            grad_ref[pl.ds(first * width_x + index, ROWS, stride=width_x), :] = (
                sum_ref[here, rows, :] + lam * curve_ref[here, rows, :]
            )

    over_rows(depth, step)


def shift(x, distance):
    count = lax.axis_size("sub")
    return lax.ppermute(x, "sub", [(i, (i + distance) % count) for i in range(count)])


def per_device(
    model,
    anchor_x,
    anchor_y,
    state_before,
    state_now,
    adjoint_later,
    adjoint_latest,
    wavelet,
    src_index,
    rec_index,
    observed,
):
    groups = lax.axis_size("shots")
    slabs = lax.axis_size("sub")
    _, model_x, model_y = model.shape
    depth, width_x, width_y = state_now.shape[1:]
    across = width_x * slabs
    block = depth * width_x
    me = lax.axis_index("sub").astype(jnp.int32)[None]
    weights = band(width_y)
    f32 = jnp.float32

    def shape(*dims):
        return jax.ShapeDtypeStruct(dims, f32)

    state = pltpu.VMEM((depth, width_x, width_y), jnp.bfloat16)
    fields, panels = pl.pallas_call(
        functools.partial(first_kernel, groups, depth, width_x),
        out_shape=[shape(4 * block, width_y), shape(groups * width_x, width_y)],
        in_specs=[SMEM] + [HBM] * 7,
        out_specs=[HBM] * 2,
        scratch_shapes=[pltpu.VMEM((model_x, width_y), f32)] * 2
        + [state] * 4
        + [
            pltpu.VMEM((depth, width_x, width_y), f32),
            pltpu.VMEM((4 * block, width_y), f32),
            pltpu.VMEM((groups * width_x, width_y), f32),
            pltpu.SMEM((groups,), jnp.int32),
            pltpu.SMEM((groups,), jnp.int32),
            pltpu.SemaphoreType.DMA((8,)),
            pltpu.SemaphoreType.DMA((2,)),
        ],
        name="first",
    )(me, anchor_x, anchor_y, model[0], state_before[0], state_now[0], adjoint_later[0], adjoint_latest[0])
    left = shift(fields, 1)
    right = shift(fields, -1)
    extra = pl.pallas_call(
        functools.partial(receiver_kernel, rec_index.shape[1], across, depth),
        out_shape=shape(across * depth * 4, width_y),
        in_specs=[HBM, HBM],
        out_specs=VMEM,
        scratch_shapes=[
            pltpu.SMEM((1, rec_index.shape[1]), jnp.int32),
            pltpu.SMEM((STEPS, 1, rec_index.shape[1]), f32),
            pltpu.SemaphoreType.DMA((2,)),
        ],
        name="receivers",
    )(rec_index, jnp.transpose(observed, (1, 0, 2)))

    far_a = shift(left[: 2 * block], 1)
    far_b = shift(right[2 * block :], -1)

    speed = lax.all_to_all(
        panels.reshape(groups, width_x, width_y), "shots", split_axis=0, concat_axis=0, tiled=True
    ).reshape(block, width_y)

    whole = (across, depth, width_y)
    padded = (across + 2 * REACH, depth, width_y)
    start, push, late, back, curve = pl.pallas_call(
        functools.partial(before_kernel, slabs, depth, width_x),
        out_shape=[shape(*padded)] + [shape(*whole)] * 4,
        in_specs=[SMEM] + [HBM] * 5 + [VMEM],
        out_specs=[VMEM] * 5,
        scratch_shapes=[pltpu.VMEM((width_x, depth, width_y), f32), pltpu.SemaphoreType.DMA((4,))],
        compiler_params=PARAMS,
        name="before",
    )(me, *(piece.reshape(-1, depth, width_y) for piece in (fields, left, right, far_a, far_b)), weights)

    speed, extra = lax.optimization_barrier((speed, extra))
    speed_left = shift(speed, 1)
    speed_right = shift(speed, -1)
    speed_far = shift(speed, 2)

    slab = jax.ShapeDtypeStruct((width_x, depth, width_y), jnp.bfloat16)
    grad, first, second = pl.pallas_call(
        functools.partial(main_kernel, slabs, depth, width_x),
        out_shape=[shape(block, width_y), slab, slab],
        in_specs=[SMEM] * 3 + [VMEM] * 9 + [HBM, VMEM],
        out_specs=[VMEM] * 3,
        scratch_shapes=[
            pltpu.VMEM(whole, f32),
            pltpu.VMEM(padded, f32),
            pltpu.VMEM(padded, f32),
            pltpu.VMEM(padded, f32),
            pltpu.VMEM(padded, f32),
            pltpu.VMEM(whole, f32),
            pltpu.VMEM(whole, f32),
            pltpu.VMEM(whole, f32),
            pltpu.VMEM(whole, f32),
            pltpu.VMEM((depth, width_y), f32),
            pltpu.VMEM((width_x, depth, width_y), f32),
            pltpu.VMEM((width_x, depth, width_y), f32),
            pltpu.VMEM((across * depth * 4, width_y), f32),
            pltpu.SemaphoreType.DMA,
        ],
        compiler_params=PARAMS,
        name="window",
    )(
        me, src_index, wavelet, speed, speed_left, speed_right, speed_far,
        start, push, late, back, curve, extra, weights,
    )

    returned = lax.all_to_all(
        grad.reshape(groups, width_x, width_y), "shots", split_axis=0, concat_axis=0, tiled=True
    ).reshape(groups * width_x, width_y)
    owned = pl.pallas_call(
        functools.partial(spread_kernel, groups, width_x),
        out_shape=shape(model_x, model_y),
        in_specs=[SMEM, SMEM, SMEM, VMEM],
        out_specs=VMEM,
        scratch_shapes=[pltpu.VMEM((model_x, width_y), f32)] * 8,
        compiler_params=PARAMS,
        name="spread",
    )(me, anchor_x, anchor_y, returned)
    parts = lax.all_to_all(
        owned.reshape(slabs, model_x // slabs, model_y), "sub", split_axis=0, concat_axis=0, tiled=True
    )
    gradient = parts[0]
    for index in range(1, slabs):
        gradient = gradient + parts[index]
    return (
        gradient[None],
        jnp.transpose(first, (1, 0, 2))[None],
        jnp.transpose(second, (1, 0, 2))[None],
    )


def solution(mesh):
    return jax.shard_map(
        per_device,
        mesh=mesh,
        in_specs=(
            P("shots", None, None),
            P(),
            P(),
            P("shots", None, "sub", None),
            P("shots", None, "sub", None),
            P("shots", None, "sub", None),
            P("shots", None, "sub", None),
            P("shots", None),
            P("shots"),
            P("shots", None),
            P("shots", None, None),
        ),
        out_specs=(
            P("shots", "sub", None),
            P("shots", None, "sub", None),
            P("shots", None, "sub", None),
        ),
        check_vma=False,
    )
```

```python
import functools

import jax
import jax.numpy as jnp
import numpy as np
from jax import lax
from jax.experimental import pallas as pl
from jax.experimental.pallas import tpu as pltpu
from jax.sharding import PartitionSpec as P

STEPS = 3
REACH = 4
UNIT = 5040.0
WHOLE = (8064.0, -1008.0, 128.0, -9.0)
CENTRE = 3.0 * (-205.0 / 72.0)
WEIGHTS = (8.0 / 5.0, -1.0 / 5.0, 8.0 / 315.0, -1.0 / 560.0)

SMEM = pl.BlockSpec(memory_space=pltpu.SMEM)
HBM = pl.BlockSpec(memory_space=pltpu.HBM)
VMEM = pl.BlockSpec(memory_space=pltpu.VMEM)
PARAMS = pltpu.CompilerParams(vmem_limit_bytes=24 << 20)


def band(size):
    offset = np.abs(np.arange(size)[:, None] - np.arange(size)[None, :])
    matrix = np.zeros((size, size), np.float32)
    for reach, weight in enumerate(WHOLE, start=1):
        matrix[offset == reach] = weight
    return jnp.asarray(matrix, jnp.bfloat16)


ROWS = 16
GROUP = 2


def along(ref, x, count, band_ref, part_ref):
    weights = band_ref[...]
    twice_down = jnp.concatenate([weights, weights], axis=0)
    twice_across = jnp.concatenate([weights, weights], axis=1)
    for index in range(0, count, 2):
        highs, lows = [], []
        for slice_x in (x + REACH + index, x + REACH + index + 1):
            centre = ref[slice_x]
            highs.append(centre.astype(jnp.bfloat16))
            lows.append((centre - highs[-1].astype(jnp.float32)).astype(jnp.bfloat16))
        beside = [jnp.concatenate(pair, axis=1) for pair in zip(highs, lows)]
        along_y = jnp.dot(jnp.concatenate(beside, axis=0), twice_down, preferred_element_type=jnp.float32)
        above = jnp.concatenate([jnp.concatenate(highs, axis=1), jnp.concatenate(lows, axis=1)], axis=0)
        along_z = jnp.dot(twice_across, above, preferred_element_type=jnp.float32)
        size = weights.shape[0]
        part_ref[index] = along_y[:size] + along_z[:, :size]
        part_ref[index + 1] = along_y[size:] + along_z[:, size:]


def laplace(ref, x, count, rows, part_ref):
    near = [ref[x + index, rows, :] for index in range(count + 2 * REACH)]
    totals = []
    for index in range(count):
        centre = index + REACH
        total = CENTRE * near[centre] + part_ref[index, rows, :] * (1.0 / UNIT)
        for reach, weight in enumerate(WEIGHTS, start=1):
            total = total + weight * (near[centre - reach] + near[centre + reach])
        totals.append(total)
    return totals


def over_rows(depth, step):
    def body(index, carry):
        step(pl.ds(pl.multiple_of(index * ROWS, ROWS), ROWS), pl.multiple_of(index * ROWS, ROWS))
        return carry

    lax.fori_loop(0, depth // ROWS, body, 0, unroll=8)


def spread_kernel(shots, width_x, me_ref, ax_ref, ay_ref, in_ref, out_ref, *sum_refs):
    width_y = in_ref.shape[1]
    first = me_ref[0] * width_x
    for ref in sum_refs:
        ref[...] = jnp.zeros_like(ref)
    lane = lax.broadcasted_iota(jnp.int32, (width_x, width_y), 1)
    pairs = [sum_refs[index : index + 2] for index in range(0, len(sum_refs), 2)]

    def body(group, carry):
        for member, (near_ref, far_ref) in enumerate(pairs):
            shot = group * len(pairs) + member
            start = pl.multiple_of(shot * width_x, width_x)
            column = ay_ref[shot]
            moved = pltpu.roll(in_ref[pl.ds(start, width_x), :], lax.rem(column, width_y), 1)
            rows = pl.ds(ax_ref[shot] + first, width_x)
            near_ref[rows, :] = near_ref[rows, :] + jnp.where(lane < column, 0.0, moved)
            far_ref[rows, :] = far_ref[rows, :] + jnp.where(lane < column, moved, 0.0)
        return carry

    lax.fori_loop(0, shots // len(pairs), body, 0, unroll=16)
    out_ref[:, :width_y] = sum(ref[...] for ref, _ in pairs)
    out_ref[:, width_y:] = sum(ref[...] for _, ref in pairs)


def cell(flat, across, width_y):
    shift_y = width_y.bit_length() - 1
    shift_x = across.bit_length() - 1
    row = lax.shift_right_logical(flat, shift_y)
    return lax.shift_right_logical(row, shift_x), row & (across - 1), flat & (width_y - 1)


def receiver_kernel(count, across, depth, index_hbm, seen_hbm, out_ref, index_ref, seen_ref, sems):
    width_y = out_ref.shape[1]
    load_index = pltpu.make_async_copy(index_hbm, index_ref, sems.at[0])
    load_seen = pltpu.make_async_copy(seen_hbm, seen_ref, sems.at[1])
    load_index.start()
    load_seen.start()
    out_ref[...] = jnp.zeros_like(out_ref)
    load_index.wait()
    load_seen.wait()
    shape = (4, width_y)
    lane = lax.broadcasted_iota(jnp.int32, shape, 1)
    line = lax.broadcasted_iota(jnp.int32, shape, 0)

    def body(group, carry):
        starts, sums = [], []
        for member in range(GROUP):
            receiver = group * GROUP + member
            cell_z, cell_x, cell_y = cell(index_ref[0, receiver], across, width_y)
            value = jnp.where(line == 1, seen_ref[0, 0, receiver], 1.0)
            value = jnp.where(line == 2, seen_ref[1, 0, receiver], value)
            value = jnp.where(line == 3, seen_ref[2, 0, receiver], value)
            start = pl.multiple_of((cell_x * depth + cell_z) * 4, 4)
            tile = out_ref[pl.ds(start, 4), :]
            for earlier, total in zip(starts, sums):
                tile = jnp.where(earlier == start, total, tile)
            starts.append(start)
            sums.append(tile + jnp.where(lane == cell_y, value, 0.0))
        for start, total in zip(starts, sums):
            out_ref[pl.ds(start, 4), :] = total
        return carry

    lax.fori_loop(0, count // GROUP, body, 0, unroll=16)


def fields_kernel(
    depth, width_x, before_hbm, now_hbm, later_hbm, latest_hbm, out_ref, before_ref, now_ref, later_ref, latest_ref, turn_ref, sems
):
    block = depth * width_x
    width_y = out_ref.shape[1]
    pairs = ((now_hbm, now_ref), (before_hbm, before_ref), (later_hbm, later_ref), (latest_hbm, latest_ref))
    loads = [pltpu.make_async_copy(source, ref, sems.at[k]) for k, (source, ref) in enumerate(pairs)]
    for load in loads:
        load.start()

    def put(place, value):
        turn_ref[...] = value
        flat = turn_ref.reshape(block, width_y)
        for row in range(width_x):
            out_ref[pl.ds(place * block + row * depth, depth), :] = flat[pl.ds(row, depth, stride=width_x), :]

    for load in loads:
        load.wait()
    now = now_ref[...].astype(jnp.float32)
    put(0, now)
    put(1, 2.0 * now - before_ref[...].astype(jnp.float32))
    later = later_ref[...].astype(jnp.float32)
    put(2, later)
    put(3, 2.0 * later - latest_ref[...].astype(jnp.float32))


def cut_kernel(shots, width_x, me_ref, ax_hbm, ay_hbm, model_hbm, out_ref, near_ref, far_ref, ax_ref, ay_ref, sems):
    width_y = out_ref.shape[1]
    pairs = (
        (model_hbm.at[:, :width_y], near_ref),
        (model_hbm.at[:, width_y:], far_ref),
        (ax_hbm, ax_ref),
        (ay_hbm, ay_ref),
    )
    loads = [pltpu.make_async_copy(source, ref, sems.at[k]) for k, (source, ref) in enumerate(pairs)]
    for load in loads:
        load.start()
    for load in loads:
        load.wait()
    first = me_ref[0] * width_x
    lane = lax.broadcasted_iota(jnp.int32, (width_x, width_y), 1)

    def cut(shot, carry):
        rows = pl.ds(ax_ref[shot] + first, width_x)
        column = ay_ref[shot]
        turn = lax.rem(2 * width_y - column, width_y)
        near = pltpu.roll(near_ref[rows, :], turn, 1)
        far = pltpu.roll(far_ref[rows, :], turn, 1)
        start = pl.multiple_of(shot * width_x, width_x)
        out_ref[pl.ds(start, width_x), :] = jnp.where(lane < width_y - column, near, far)
        return carry

    lax.fori_loop(0, shots, cut, 0, unroll=128)


def slab_slice(ref, first, depth, width_x, row):
    return ref[pl.ds(first + row, depth, stride=width_x), :]


def before_kernel(
    slabs, depth, width_x, me_ref, own_ref, left_ref, right_ref, far_a_ref, far_b_ref, band_ref,
    start_ref, push_ref, later_ref, back_ref, curve_ref, part_ref, sems,
):
    me = me_ref[0]
    across = slabs * width_x
    outs = (start_ref, push_ref, later_ref, back_ref)
    copies = []
    for distance, pieces in (
        (0, [(own_ref, k) for k in range(4)]),
        (slabs - 1, [(left_ref, k) for k in range(4)]),
        (1, [(right_ref, k) for k in range(4)]),
        (2, [(far_a_ref, 0), (far_a_ref, 1), (far_b_ref, 0), (far_b_ref, 1)]),
    ):
        base = lax.rem(me + distance, slabs) * width_x
        for field, ((ref, place), out) in enumerate(zip(pieces, outs)):
            offset = REACH if field == 0 else 0
            source = ref.at[pl.ds(place * width_x, width_x)]
            target = out.at[pl.ds(base + offset, width_x)]
            copies.append((field, pltpu.make_async_copy(source, target, sems.at[field])))
    copies.sort(key=lambda item: item[0])
    for _, copy in copies:
        copy.start()
    zeros = jnp.zeros(start_ref.shape[1:], jnp.float32)
    for row in range(REACH):
        start_ref[row] = zeros
        start_ref[REACH + across + row] = zeros
    for field, copy in copies:
        if field == 0:
            copy.wait()

    def curve(slab, carry):
        x = slab * width_x
        along(start_ref, x, width_x, band_ref, part_ref)

        def step(rows, _):
            for index, bend in enumerate(laplace(start_ref, x, width_x, rows, part_ref)):
                curve_ref[x + index, rows, :] = bend

        over_rows(depth, step)
        return carry

    lax.fori_loop(0, slabs, curve, 0)
    for field, copy in copies:
        if field:
            copy.wait()


def main_kernel(
    slabs, depth, width_x, me_ref, source_ref, wave_ref, own_ref, left_ref, right_ref, far_ref,
    start_ref, push_ref, later_ref, back_ref, curve_ref, extra_hbm, band_ref,
    grad_ref, first_ref, second_ref,
    speed_ref, one_ref, two_ref, scaled_ref, again_ref, curve_one_ref, lam_ref, lam_two_ref, sum_ref, mark_ref,
    part_ref, other_ref, extra_ref, extra_sem,
):
    me = me_ref[0]
    across = slabs * width_x
    width_y = mark_ref.shape[1]
    load_extra = pltpu.make_async_copy(extra_hbm, extra_ref, extra_sem)
    load_extra.start()
    for distance, ref in ((0, own_ref), (slabs - 1, left_ref), (1, right_ref), (2, far_ref)):
        base = lax.rem(me + distance, slabs) * width_x
        for row in range(width_x):
            speed_ref[base + row] = slab_slice(ref, 0, depth, width_x, row)
    zeros = jnp.zeros((depth, width_y), jnp.float32)
    for ref in (one_ref, two_ref, scaled_ref, again_ref):
        for row in range(REACH):
            ref[row] = zeros
            ref[REACH + across + row] = zeros
    source_z, source_x, source_y = cell(source_ref[0], across, width_y)
    spot_z = lax.broadcasted_iota(jnp.int32, (depth, width_y), 0) == source_z
    spot_y = lax.broadcasted_iota(jnp.int32, (depth, width_y), 1) == source_y
    mark_ref[...] = jnp.where(spot_z & spot_y, 1.0, 0.0)

    def add_source(ref, step):
        row = pl.ds(source_z, 1)
        lane = lax.broadcasted_iota(jnp.int32, (1, width_y), 1)
        pulse = jnp.where(lane == source_y, wave_ref[0, step], 0.0)
        ref[source_x + REACH, row, :] = ref[source_x + REACH, row, :] + pulse

    def pulse(x, step, rows):
        return mark_ref[rows, :] * jnp.where(x == source_x, wave_ref[0, step], 0.0)

    def extra(x, line, first):
        return extra_ref[pl.ds((x * depth + first) * 4 + line, ROWS, stride=4), :]

    def by_slabs(step, slices):
        low = jnp.maximum(me - slices // width_x, 0)
        high = jnp.minimum(me + 1 + slices // width_x, slabs)

        def body(slab, carry):
            step(slab * width_x)
            return carry

        lax.fori_loop(low, high, body, 0)

    def step_one(x):
        def step(rows, _):
            for here in range(width_x):
                here = x + here
                speed = speed_ref[here, rows, :]
                one_ref[here + REACH, rows, :] = (
                    push_ref[here, rows, :] + speed * curve_ref[here, rows, :]
                )
                scaled_ref[here + REACH, rows, :] = speed * later_ref[here, rows, :]

        over_rows(depth, step)

    for slab in range(slabs):
        step_one(slab * width_x)
    add_source(one_ref, 0)

    def step_two(x):
        part = part_ref if x // width_x % 2 else other_ref
        along(one_ref, x, width_x, band_ref, part)

        def step(rows, _):
            for index, bend in enumerate(laplace(one_ref, x, width_x, rows, part)):
                here = x + index
                curve_one_ref[here, rows, :] = bend
                two_ref[here + REACH, rows, :] = (
                    2.0 * one_ref[here + REACH, rows, :]
                    - start_ref[here + REACH, rows, :]
                    + speed_ref[here, rows, :] * bend
                )

        over_rows(depth, step)

    for slab in range(slabs):
        step_two(slab * width_x)
    add_source(two_ref, 1)

    def back_three(x):
        along(two_ref, x, width_x, band_ref, part_ref)
        along(scaled_ref, x, width_x, band_ref, other_ref)

        def step(rows, first):
            bends = laplace(two_ref, x, width_x, rows, part_ref)
            backs = laplace(scaled_ref, x, width_x, rows, other_ref)
            for index, (bend, back) in enumerate(zip(bends, backs)):
                here = x + index
                speed = speed_ref[here, rows, :]
                three = (
                    2.0 * two_ref[here + REACH, rows, :]
                    - one_ref[here + REACH, rows, :]
                    + speed * bend
                    + pulse(here, 2, rows)
                )
                lam = back_ref[here, rows, :] + back
                lam = lam + (extra(here, 0, first) * three - extra(here, 3, first))
                lam_ref[here, rows, :] = lam
                sum_ref[here, rows, :] = lam * bend
                again_ref[here + REACH, rows, :] = speed * lam

        over_rows(depth, step)

    load_extra.wait()
    by_slabs(back_three, 2 * REACH)

    def back_two(x):
        along(again_ref, x, width_x, band_ref, part_ref)

        def step(rows, first):
            for index, back in enumerate(laplace(again_ref, x, width_x, rows, part_ref)):
                here = x + index
                lam = 2.0 * lam_ref[here, rows, :] - later_ref[here, rows, :] + back
                lam = lam + (extra(here, 0, first) * two_ref[here + REACH, rows, :] - extra(here, 2, first))
                lam_two_ref[here, rows, :] = lam
                sum_ref[here, rows, :] = sum_ref[here, rows, :] + lam * curve_one_ref[here, rows, :]
                scaled_ref[here + REACH, rows, :] = speed_ref[here, rows, :] * lam

        over_rows(depth, step)

    by_slabs(back_two, REACH)

    x = me * width_x
    along(scaled_ref, x, width_x, band_ref, part_ref)

    def step(rows, first):
        for index, back in enumerate(laplace(scaled_ref, x, width_x, rows, part_ref)):
            here = x + index
            lam_two = lam_two_ref[here, rows, :]
            lam = 2.0 * lam_two - lam_ref[here, rows, :] + back
            lam = lam + (extra(here, 0, first) * one_ref[here + REACH, rows, :] - extra(here, 1, first))
            first_ref[index, rows, :] = lam.astype(first_ref.dtype)
            second_ref[index, rows, :] = lam_two.astype(second_ref.dtype)
            grad_ref[pl.ds(first * width_x + index, ROWS, stride=width_x), :] = (
                sum_ref[here, rows, :] + lam * curve_ref[here, rows, :]
            )

    over_rows(depth, step)


def shift(x, distance):
    count = lax.axis_size("sub")
    return lax.ppermute(x, "sub", [(i, (i + distance) % count) for i in range(count)])


def per_device(
    model,
    anchor_x,
    anchor_y,
    state_before,
    state_now,
    adjoint_later,
    adjoint_latest,
    wavelet,
    src_index,
    rec_index,
    observed,
):
    groups = lax.axis_size("shots")
    slabs = lax.axis_size("sub")
    _, model_x, model_y = model.shape
    depth, width_x, width_y = state_now.shape[1:]
    across = width_x * slabs
    block = depth * width_x
    me = lax.axis_index("sub").astype(jnp.int32)[None]
    weights = band(width_y)
    f32 = jnp.float32

    def shape(*dims):
        return jax.ShapeDtypeStruct(dims, f32)

    state = pltpu.VMEM((depth, width_x, width_y), jnp.bfloat16)
    fields = pl.pallas_call(
        functools.partial(fields_kernel, depth, width_x),
        out_shape=shape(4 * block, width_y),
        in_specs=[HBM] * 4,
        out_specs=VMEM,
        scratch_shapes=[state] * 4
        + [pltpu.VMEM((depth, width_x, width_y), f32), pltpu.SemaphoreType.DMA((4,))],
        name="fields",
    )(state_before[0], state_now[0], adjoint_later[0], adjoint_latest[0])
    panels = pl.pallas_call(
        functools.partial(cut_kernel, groups, width_x),
        out_shape=shape(groups * width_x, width_y),
        in_specs=[SMEM] + [HBM] * 3,
        out_specs=VMEM,
        scratch_shapes=[pltpu.VMEM((model_x, width_y), f32)] * 2
        + [pltpu.SMEM((groups,), jnp.int32)] * 2
        + [pltpu.SemaphoreType.DMA((4,))],
        name="cut",
    )(me, anchor_x, anchor_y, model[0])
    left = shift(fields, 1)
    right = shift(fields, -1)
    extra = pl.pallas_call(
        functools.partial(receiver_kernel, rec_index.shape[1], across, depth),
        out_shape=shape(across * depth * 4, width_y),
        in_specs=[HBM, HBM],
        out_specs=VMEM,
        scratch_shapes=[
            pltpu.SMEM((1, rec_index.shape[1]), jnp.int32),
            pltpu.SMEM((STEPS, 1, rec_index.shape[1]), f32),
            pltpu.SemaphoreType.DMA((2,)),
        ],
        name="receivers",
    )(rec_index, jnp.transpose(observed, (1, 0, 2)))

    far_a = shift(left[: 2 * block], 1)
    far_b = shift(right[2 * block :], -1)

    speed = lax.all_to_all(
        panels.reshape(groups, width_x, width_y), "shots", split_axis=0, concat_axis=0, tiled=True
    ).reshape(block, width_y)

    whole = (across, depth, width_y)
    padded = (across + 2 * REACH, depth, width_y)
    start, push, late, back, curve = pl.pallas_call(
        functools.partial(before_kernel, slabs, depth, width_x),
        out_shape=[shape(*padded)] + [shape(*whole)] * 4,
        in_specs=[SMEM] + [HBM] * 5 + [VMEM],
        out_specs=[VMEM] * 5,
        scratch_shapes=[pltpu.VMEM((width_x, depth, width_y), f32), pltpu.SemaphoreType.DMA((4,))],
        compiler_params=PARAMS,
        name="before",
    )(me, *(piece.reshape(-1, depth, width_y) for piece in (fields, left, right, far_a, far_b)), weights)

    speed, extra = lax.optimization_barrier((speed, extra))
    speed_left = shift(speed, 1)
    speed_right = shift(speed, -1)
    speed_far = shift(speed, 2)

    slab = jax.ShapeDtypeStruct((width_x, depth, width_y), jnp.bfloat16)
    grad, first, second = pl.pallas_call(
        functools.partial(main_kernel, slabs, depth, width_x),
        out_shape=[shape(block, width_y), slab, slab],
        in_specs=[SMEM] * 3 + [VMEM] * 9 + [HBM, VMEM],
        out_specs=[VMEM] * 3,
        scratch_shapes=[
            pltpu.VMEM(whole, f32),
            pltpu.VMEM(padded, f32),
            pltpu.VMEM(padded, f32),
            pltpu.VMEM(padded, f32),
            pltpu.VMEM(padded, f32),
            pltpu.VMEM(whole, f32),
            pltpu.VMEM(whole, f32),
            pltpu.VMEM(whole, f32),
            pltpu.VMEM(whole, f32),
            pltpu.VMEM((depth, width_y), f32),
            pltpu.VMEM((width_x, depth, width_y), f32),
            pltpu.VMEM((width_x, depth, width_y), f32),
            pltpu.VMEM((across * depth * 4, width_y), f32),
            pltpu.SemaphoreType.DMA,
        ],
        compiler_params=PARAMS,
        name="window",
    )(
        me, src_index, wavelet, speed, speed_left, speed_right, speed_far,
        start, push, late, back, curve, extra, weights,
    )

    returned = lax.all_to_all(
        grad.reshape(groups, width_x, width_y), "shots", split_axis=0, concat_axis=0, tiled=True
    ).reshape(groups * width_x, width_y)
    owned = pl.pallas_call(
        functools.partial(spread_kernel, groups, width_x),
        out_shape=shape(model_x, model_y),
        in_specs=[SMEM, SMEM, SMEM, VMEM],
        out_specs=VMEM,
        scratch_shapes=[pltpu.VMEM((model_x, width_y), f32)] * 8,
        compiler_params=PARAMS,
        name="spread",
    )(me, anchor_x, anchor_y, returned)
    parts = lax.all_to_all(
        owned.reshape(slabs, model_x // slabs, model_y), "sub", split_axis=0, concat_axis=0, tiled=True
    )
    gradient = parts[0]
    for index in range(1, slabs):
        gradient = gradient + parts[index]
    return (
        gradient[None],
        jnp.transpose(first, (1, 0, 2))[None],
        jnp.transpose(second, (1, 0, 2))[None],
    )


def solution(mesh):
    return jax.shard_map(
        per_device,
        mesh=mesh,
        in_specs=(
            P("shots", None, None),
            P(),
            P(),
            P("shots", None, "sub", None),
            P("shots", None, "sub", None),
            P("shots", None, "sub", None),
            P("shots", None, "sub", None),
            P("shots", None),
            P("shots"),
            P("shots", None),
            P("shots", None, None),
        ),
        out_specs=(
            P("shots", "sub", None),
            P("shots", None, "sub", None),
            P("shots", None, "sub", None),
        ),
        check_vma=False,
    )
```
